32 devices in a mesh: groups: 2 (over y), dap: 4 (over z), branch: 2 (over x), chan: 2 (over core).
Axes of the slice: x: 2, y: 2, z: 4, core: 2. Of those that a mesh axis runs over, the one named last changes fastest.
Arguments:
- homolog_features: bfloat16 [128, 128, 256], P(('groups', 'dap', 'branch', 'chan')), parts along dimension 0, may hold values from -0.14941406 to 0.14941406
- alignment_tokens: int32 [128, 128], P(('groups', 'dap', 'branch', 'chan')), parts along dimension 0, may hold values from 0 to 22
- alignment_mask: int32 [128, 128], P(('groups', 'dap', 'branch', 'chan')), parts along dimension 0, may hold values 0 or 1
- pair_activation_input: bfloat16 [256, 128, 128], P(('groups', 'dap'), ('branch', 'chan')), parts along dimension 0, may hold values from -6 to 6
- pair_residue_mask: int32 [256, 128], P(('groups', 'dap'), ('branch', 'chan')), parts along dimension 0, may hold values 0 or 1
- letter_lookup_matrix: bfloat16 [23, 256], replicated, may hold values from -0.14941406 to 0.14941406
- homolog_focus_scaling: float32 [256], replicated, may hold values from 0.5 to 1.5
- focus_entry_matrix: bfloat16 [256, 1024], replicated, may hold values from -0.375 to 0.375
- focus_exit_matrix: bfloat16 [256, 256], replicated, may hold values from -0.375 to 0.375
- pair_norm_gain: float32 [128], replicated, may hold values from 0.5 to 1.5
- head_bias_weight: bfloat16 [128, 8], replicated, may hold values from -40 to 40
- tensor_product_scaling: float32 [256], replicated, may hold values from 0.5 to 1.5
- tensor_product_matrix: bfloat16 [256, 64], replicated, may hold values from -0.375 to 0.375
- outer_output_weight: bfloat16 [1024, 128], replicated, may hold values from -1.5 to 1.5
- triangle_input_weight: bfloat16 [128, 640], replicated, may hold values from -0.5 to 0.5
- triangle_norm_gain: float32 [128], replicated, may hold values from 0.5 to 1.5
- triangle_output_weight: bfloat16 [128, 128], replicated, may hold values from -0.5 to 0.5
Outputs:
- alignment_output: bfloat16 [128, 128, 256], P(('groups', 'dap', 'branch', 'chan')), parts along dimension 0
- pair_activation_output: bfloat16 [256, 128, 128], P(('groups', 'dap'), ('branch', 'chan')), parts along dimension 0
The draws below stay inside these ranges and needn't reach their ends.
There are 2 independent parts, one for each index of `groups`. The reference program is written for one: setup_inputs(seed, part) draws one part's arguments, and reference() takes and returns one part's arrays. A program takes and returns all parts, laid end to end along the dimension named above; an argument that names none is the same for every part. Nothing has to cross between parts.
All inputs are finite; a program needn't handle non-finite values. No bound on the sum of `alignment_mask` or of `pair_residue_mask` on one device may be relied on, other than what follows from the above.
Results may differ from the reference program's by a relative error of at most 0.011.
The reference program's roundings to bfloat16 on the way count: a program that leaves them out, or rounds other values in their place, can miss the bound.
Values may be sent and summed in bfloat16 or wider, within the bound.
A program may use at most 128 MiB of HBM per device.

```python
import math
import jax
import jax.numpy as jnp
from jax import lax

FEATURE_DEPTH = 256
CZ = 128
HEADS = 8
PRODUCT_DEPTH = 32
LETTER_KINDS = 23
HOMOLOG_TALLY = 64
CROP_LENGTH = 128
N_DAP = 4


def draw_head_bias_weight(key, part):
    key_base, key_scale = jax.random.split(key, 2)
    base = jax.random.normal(key_base, (CZ, HEADS), jnp.float32) * CZ ** (-0.5)
    scales = jnp.exp(jax.random.uniform(key_scale, (HEADS,), jnp.float32, math.log(0.5), math.log(1.5)))
    return jnp.clip(base * scales[None, :], -40.0, 40.0).astype(jnp.bfloat16)


def touch_ends(entries, stream_key, smallest, largest):
    spot = [jax.random.randint(jax.random.fold_in(stream_key, axis), (), 0, length) for axis, length in enumerate(entries.shape)]
    main_axis = entries.shape.index(max(entries.shape))
    neighbour = spot[:main_axis] + [(spot[main_axis] + 1) % entries.shape[main_axis]] + spot[main_axis + 1:]
    return entries.at[tuple(spot)].set(smallest).at[tuple(neighbour)].set(largest)


def shard_levels(stream_key, extent, cuts, low, high):
    loudness = 1.0
    for axis_at, shards_of in cuts:
        heights = jax.random.uniform(jax.random.fold_in(jax.random.fold_in(stream_key, 6), axis_at), (shards_of,), jnp.float32, low / len(cuts), high / len(cuts))
        loudness = loudness * jnp.repeat(jnp.exp(heights), extent[axis_at] // shards_of).reshape((-1,) + (1,) * (len(extent) - 1 - axis_at))
    return loudness


def centred(key, dims, deviation, reach, cuts=(), kind=jnp.bfloat16):
    array = jax.random.normal(key, dims, jnp.float32) * deviation
    if len(cuts) > 0:
        array = shard_levels(key, dims, cuts, -0.22, 0.18) * array
    return jnp.clip(array, min=-reach, max=reach).astype(kind)


def setup_inputs(seed: int = 0, part: int = 0) -> dict:
    splits = jax.random.split(jax.random.key(seed), 18)
    part_splits = jax.random.split(jax.random.fold_in(splits[17], part), 18)
    return {
        "homolog_features": jnp.clip(jax.random.uniform(part_splits[0], (HOMOLOG_TALLY, CROP_LENGTH, FEATURE_DEPTH), jnp.float32, -0.14941406, 0.14941406) * shard_levels(part_splits[0], (HOMOLOG_TALLY, CROP_LENGTH, FEATURE_DEPTH), ((0, 16),), -0.4, 0.0), -0.14941406, 0.14941406).astype(jnp.bfloat16),
        "alignment_tokens": touch_ends(jax.random.randint(part_splits[1], (HOMOLOG_TALLY, CROP_LENGTH), 0, LETTER_KINDS), jax.random.fold_in(part_splits[1], 1), 0, LETTER_KINDS - 1).astype(jnp.int32),
        "alignment_mask": touch_ends((jax.random.randint(part_splits[2], (HOMOLOG_TALLY, CROP_LENGTH), 0, 8) < 7).astype(jnp.int32), jax.random.fold_in(part_splits[2], 1), 0, 1),
        "pair_activation_input": centred(part_splits[3], (CROP_LENGTH, CROP_LENGTH, CZ), 1.0, 6.0, ((0, 4), (1, 4))),
        "pair_residue_mask": touch_ends((jax.random.randint(part_splits[4], (CROP_LENGTH, CROP_LENGTH), 0, 8) < 7).astype(jnp.int32), jax.random.fold_in(part_splits[4], 1), 0, 1),
        "letter_lookup_matrix": jnp.clip(jax.random.uniform(splits[5], (LETTER_KINDS, FEATURE_DEPTH), jnp.float32, -0.14941406, 0.14941406), -0.14941406, 0.14941406).astype(jnp.bfloat16),
        "homolog_focus_scaling": jnp.clip(1.0 + 0.1 * jax.random.normal(splits[6], (FEATURE_DEPTH,), jnp.float32), 0.5, 1.5),
        "focus_entry_matrix": centred(splits[7], (FEATURE_DEPTH, 4 * FEATURE_DEPTH), FEATURE_DEPTH ** -0.5, 0.375),
        "focus_exit_matrix": centred(splits[8], (FEATURE_DEPTH, FEATURE_DEPTH), FEATURE_DEPTH ** -0.5, 0.375),
        "pair_norm_gain": jnp.clip(1.0 + 0.1 * jax.random.normal(splits[9], (CZ,), jnp.float32), 0.5, 1.5),
        "head_bias_weight": draw_head_bias_weight(jax.random.fold_in(splits[17], 71), part),
        "tensor_product_scaling": jnp.clip(1.0 + 0.1 * jax.random.normal(splits[11], (FEATURE_DEPTH,), jnp.float32), 0.5, 1.5),
        "tensor_product_matrix": centred(splits[12], (FEATURE_DEPTH, 2 * PRODUCT_DEPTH), FEATURE_DEPTH ** -0.5, 0.375),
        "outer_output_weight": centred(splits[13], (PRODUCT_DEPTH * PRODUCT_DEPTH, CZ), (max(1, PRODUCT_DEPTH * PRODUCT_DEPTH // HOMOLOG_TALLY)) ** -0.5, 1.5),
        "triangle_input_weight": centred(splits[14], (CZ, 5 * CZ), CZ ** -0.5, 0.5),
        "triangle_norm_gain": jnp.clip(1.0 + 0.1 * jax.random.normal(splits[15], (CZ,), jnp.float32), 0.5, 1.5),
        "triangle_output_weight": centred(splits[16], (CZ, CZ), CZ ** -0.5, 0.5),
    }


def layer_normalize(values, gain_vector, norm_axis):
    center = values - lax.optimization_barrier(jnp.mean(values, axis=norm_axis, keepdims=True))
    spread = lax.optimization_barrier(jnp.mean(center * center, axis=norm_axis, keepdims=True))
    return center * lax.rsqrt(spread + 1e-05) * gain_vector

def reference(homolog_features, alignment_tokens, alignment_mask, pair_activation_input, pair_residue_mask, letter_lookup_matrix, homolog_focus_scaling, focus_entry_matrix, focus_exit_matrix, pair_norm_gain, head_bias_weight, tensor_product_scaling, tensor_product_matrix, outer_output_weight, triangle_input_weight, triangle_norm_gain, triangle_output_weight):
    sequence_total, residue_total, alignment_width = homolog_features.shape
    pair_width = pair_activation_input.shape[2]
    number_heads = head_bias_weight.shape[1]
    per_head_width = alignment_width // number_heads
    outer_factor_width = tensor_product_matrix.shape[1] // 2
    pair_normed = layer_normalize(pair_activation_input.astype(jnp.float32), pair_norm_gain.astype(jnp.float32), -1).astype(jnp.bfloat16)
    pair_bias = jnp.einsum('ijc,ch->hij', pair_normed.astype(jnp.float32), head_bias_weight.astype(jnp.float32))

    def gated_row_attention(row_item):
        act_row, token_row, mask_row = row_item
        embedded_tokens = act_row.astype(jnp.float32) + letter_lookup_matrix[token_row].astype(jnp.float32)
        normalized_values = layer_normalize(embedded_tokens, homolog_focus_scaling.astype(jnp.float32), -1).astype(jnp.bfloat16)
        projected_values = jnp.dot(normalized_values, focus_entry_matrix, preferred_element_type=jnp.float32)
        query_rows = projected_values[:, :alignment_width].astype(jnp.bfloat16).reshape(residue_total, number_heads, per_head_width)
        row_keys = projected_values[:, alignment_width:2 * alignment_width].astype(jnp.bfloat16).reshape(residue_total, number_heads, per_head_width)
        row_values = projected_values[:, 2 * alignment_width:3 * alignment_width].astype(jnp.bfloat16).reshape(residue_total, number_heads, per_head_width)
        scores = jnp.einsum('ihd,jhd->hij', query_rows.astype(jnp.float32), row_keys.astype(jnp.float32)) * per_head_width ** (-0.5) + pair_bias + (mask_row.astype(jnp.float32) - 1.0) * 1000000000.0
        attention_weights = jax.nn.softmax(scores, axis=-1).astype(jnp.bfloat16)
        attended_rows = jnp.einsum('bqo,obm->qbm', attention_weights.astype(jnp.float32), row_values.astype(jnp.float32)).reshape(residue_total, alignment_width)
        gated_output = (attended_rows * jax.nn.sigmoid(projected_values[:, 3 * alignment_width:])).astype(jnp.bfloat16)
        return (embedded_tokens + jnp.dot(gated_output, focus_exit_matrix, preferred_element_type=jnp.float32)).astype(jnp.bfloat16)
    alignment_output = lax.map(gated_row_attention, (homolog_features, alignment_tokens, alignment_mask))
    outer_normalized = layer_normalize(alignment_output.astype(jnp.float32), tensor_product_scaling.astype(jnp.float32), -1).astype(jnp.bfloat16)
    alignment_mask_rows = alignment_mask.astype(jnp.float32)[:, :, None]
    left_projection = (jnp.dot(outer_normalized, tensor_product_matrix[:, :outer_factor_width], preferred_element_type=jnp.float32) * alignment_mask_rows).astype(jnp.bfloat16)
    right_projection = (jnp.dot(outer_normalized, tensor_product_matrix[:, outer_factor_width:], preferred_element_type=jnp.float32) * alignment_mask_rows).astype(jnp.bfloat16)
    block_rows = residue_total // N_DAP

    def outer_block(block_index):
        left_block = lax.dynamic_slice_in_dim(left_projection, block_index * block_rows, block_rows, 1)
        outer = jnp.einsum('sic,sjd->ijcd', left_block.astype(jnp.float32), right_projection.astype(jnp.float32)) * (1.0 / sequence_total)
        flat_outer = outer.astype(jnp.bfloat16).reshape(block_rows, residue_total, outer_factor_width * outer_factor_width)
        return jnp.dot(flat_outer, outer_output_weight, preferred_element_type=jnp.float32)
    outer_update = lax.map(outer_block, jnp.arange(N_DAP, dtype=jnp.int32)).reshape(residue_total, residue_total, pair_width)
    tri_linear = jnp.dot(pair_normed, triangle_input_weight, preferred_element_type=jnp.float32)
    mask_pair = pair_residue_mask.astype(jnp.float32)[:, :, None]
    tri_left = (jax.nn.sigmoid(tri_linear[:, :, pair_width:2 * pair_width]) * tri_linear[:, :, :pair_width] * mask_pair).astype(jnp.bfloat16)
    tri_right = (jax.nn.sigmoid(tri_linear[:, :, 3 * pair_width:4 * pair_width]) * tri_linear[:, :, 2 * pair_width:3 * pair_width] * mask_pair).astype(jnp.bfloat16)
    tri_sum = jnp.einsum('ikc,jkc->ijc', tri_left.astype(jnp.float32), tri_right.astype(jnp.float32)).astype(jnp.bfloat16)
    tri_normed = layer_normalize(tri_sum.astype(jnp.float32), triangle_norm_gain.astype(jnp.float32), -1).astype(jnp.bfloat16)
    tri_update = jax.nn.sigmoid(tri_linear[:, :, 4 * pair_width:]) * jnp.dot(tri_normed, triangle_output_weight, preferred_element_type=jnp.float32)
    pair_activation_output = (pair_activation_input.astype(jnp.float32) + tri_update + outer_update).astype(jnp.bfloat16)
    return (alignment_output, pair_activation_output)
```

```python
import functools

import jax
import jax.numpy as jnp
from jax import lax
from jax.experimental import pallas as pl
from jax.experimental.pallas import tpu as pltpu
from jax.sharding import PartitionSpec as P


def layer_normalize(values, gain_vector, norm_axis):
    center = values - jnp.mean(values, axis=norm_axis, keepdims=True)
    spread = jnp.mean(center * center, axis=norm_axis, keepdims=True)
    return center * lax.rsqrt(spread + 1e-05) * gain_vector


def channel_products(left_part, right_part, dap_count, column_count, rows_block, column_block):
    row_ratio = dap_count // column_count
    channels_here = left_part.size // (dap_count * column_count * rows_block * column_block)
    left_five = left_part.reshape(dap_count, column_count, channels_here, rows_block, column_block)
    right_six = right_part.reshape(
        column_count, row_ratio, column_count, channels_here, rows_block, column_block
    )
    product = jnp.einsum(
        "pqrik,bhqrjk->pbrihj", left_five, right_six, preferred_element_type=jnp.float32
    )
    return product.astype(jnp.bfloat16)


def shards(
    homolog_features,
    alignment_tokens,
    alignment_mask,
    pair_activation_input,
    pair_residue_mask,
    letter_lookup_matrix,
    homolog_focus_scaling,
    focus_entry_matrix,
    focus_exit_matrix,
    pair_norm_gain,
    head_bias_weight,
    tensor_product_scaling,
    tensor_product_matrix,
    outer_output_weight,
    triangle_input_weight,
    triangle_norm_gain,
    triangle_output_weight,
):
    dap_count = lax.axis_size("dap")
    column_count = lax.axis_size("branch") * lax.axis_size("chan")
    device_count = dap_count * column_count
    rows_block, column_block, pair_width = pair_activation_input.shape
    sequence_total, residue_total, alignment_width = homolog_features.shape
    number_heads = head_bias_weight.shape[1]
    per_head_width = alignment_width // number_heads
    outer_factor_width = tensor_product_matrix.shape[1] // 2
    pair_normed = layer_normalize(
        pair_activation_input.astype(jnp.float32), pair_norm_gain, -1
    ).astype(jnp.bfloat16)
    bias_block = jnp.einsum(
        "ikc,ch->hik", pair_normed, head_bias_weight, preferred_element_type=jnp.float32
    )
    tri_linear = jnp.einsum(
        "ikc,ce->eik",
        pair_normed,
        triangle_input_weight[:, : 4 * pair_width],
        preferred_element_type=jnp.float32,
    )
    mask_pair = pair_residue_mask.astype(jnp.float32)
    tri_left = (
        jax.nn.sigmoid(tri_linear[pair_width : 2 * pair_width])
        * tri_linear[:pair_width]
        * mask_pair
    ).astype(jnp.bfloat16)
    tri_right = (
        jax.nn.sigmoid(tri_linear[3 * pair_width : 4 * pair_width])
        * tri_linear[2 * pair_width : 3 * pair_width]
        * mask_pair
    ).astype(jnp.bfloat16)
    out_gate = jnp.einsum(
        "ikc,ce->ike",
        pair_normed,
        triangle_input_weight[:, 4 * pair_width :],
        preferred_element_type=jnp.float32,
    )
    per_device = pair_width // device_count
    flat_shape = (device_count, 1, per_device, rows_block, column_block)
    products = channel_products(
        lax.all_to_all(
            tri_left.reshape(flat_shape),
            ("dap", "branch", "chan"),
            split_axis=0,
            concat_axis=1,
            tiled=True,
        ),
        lax.all_to_all(
            tri_right.reshape(flat_shape),
            ("dap", "branch", "chan"),
            split_axis=0,
            concat_axis=1,
            tiled=True,
        ),
        dap_count,
        column_count,
        rows_block,
        column_block,
    )
    channels_here = products.shape[2]
    sending = products.reshape(device_count, 1, channels_here, rows_block, column_block)
    returned = lax.all_to_all(
        sending, ("dap", "branch", "chan"), split_axis=0, concat_axis=1, tiled=True
    )
    tri_sum = returned.reshape(pair_width, rows_block, column_block)
    tri_normed = layer_normalize(
        tri_sum.astype(jnp.float32), triangle_norm_gain[:, None, None], 0
    ).astype(jnp.bfloat16)
    tri_update = jax.nn.sigmoid(out_gate) * jnp.einsum(
        "cik,ce->ike", tri_normed, triangle_output_weight, preferred_element_type=jnp.float32
    )
    token_class_count = letter_lookup_matrix.shape[0]
    token_indicator = (
        alignment_tokens[:, :, None] == jnp.arange(token_class_count, dtype=jnp.int32)
    ).astype(jnp.bfloat16)
    embedded_tokens = homolog_features.astype(jnp.float32) + jnp.einsum(
        "snv,vc->snc", token_indicator, letter_lookup_matrix, preferred_element_type=jnp.float32
    )
    alignment_normalized = layer_normalize(embedded_tokens, homolog_focus_scaling, -1).astype(
        jnp.bfloat16
    )
    projected_values = jnp.einsum(
        "rdz,zg->rdg", alignment_normalized, focus_entry_matrix, preferred_element_type=jnp.float32
    )
    query_rows = projected_values[:, :, :alignment_width].astype(jnp.bfloat16)
    every_key = projected_values[:, :, alignment_width : 2 * alignment_width].astype(jnp.bfloat16)
    every_value = projected_values[:, :, 2 * alignment_width : 3 * alignment_width].astype(
        jnp.bfloat16
    )
    gate_values = projected_values[:, :, 3 * alignment_width :]
    key_mask_bias = (alignment_mask.astype(jnp.float32) - 1.0) * 1000000000.0
    score_scale = per_head_width ** (-0.5)
    bias_partial = lax.all_gather(bias_block, ("branch", "chan"), axis=2, tiled=True)
    bias_full = lax.all_gather(bias_partial, "dap", axis=1, tiled=True)
    query_form = query_rows.reshape(sequence_total, residue_total, number_heads, per_head_width)
    key_form = every_key.reshape(sequence_total, residue_total, number_heads, per_head_width)
    value_form = every_value.reshape(sequence_total, residue_total, number_heads, per_head_width)
    mask_form = key_mask_bias.reshape(sequence_total, 1, 1, residue_total)

    def attend(seq_item):
        query_seq, key_seq, value_seq, mask_seq = seq_item
        scores = (
            jnp.einsum("ihd,jhd->hij", query_seq, key_seq, preferred_element_type=jnp.float32)
            * score_scale
            + bias_full
            + mask_seq
        )
        largest = jnp.max(scores, axis=2, keepdims=True)
        exponent = jnp.exp(scores - largest)
        attention_weights = (exponent / jnp.sum(exponent, axis=2, keepdims=True)).astype(
            jnp.bfloat16
        )
        return jnp.einsum(
            "bqo,obm->qbm", attention_weights, value_seq, preferred_element_type=jnp.float32
        )

    attended_rows = lax.map(attend, (query_form, key_form, value_form, mask_form)).reshape(
        sequence_total, residue_total, alignment_width
    )
    gated_output = (attended_rows * jax.nn.sigmoid(gate_values)).astype(jnp.bfloat16)
    alignment_output = (
        embedded_tokens
        + jnp.einsum(
            "rdz,zg->rdg", gated_output, focus_exit_matrix, preferred_element_type=jnp.float32
        )
    ).astype(jnp.bfloat16)
    outer_normalized = layer_normalize(
        alignment_output.astype(jnp.float32), tensor_product_scaling, -1
    ).astype(jnp.bfloat16)
    alignment_mask_rows = alignment_mask.astype(jnp.float32)[:, :, None]
    left_projection = (
        (
            jnp.einsum(
                "rdz,zg->rdg",
                outer_normalized,
                tensor_product_matrix[:, :outer_factor_width],
                preferred_element_type=jnp.float32,
            )
            * alignment_mask_rows
        )
        .astype(jnp.bfloat16)
        .reshape(sequence_total, residue_total * outer_factor_width)
    )
    right_projection = (
        (
            jnp.einsum(
                "rdz,zg->rdg",
                outer_normalized,
                tensor_product_matrix[:, outer_factor_width:],
                preferred_element_type=jnp.float32,
            )
            * alignment_mask_rows
        )
        .astype(jnp.bfloat16)
        .reshape(sequence_total, residue_total * outer_factor_width)
    )
    left_gathered, right_gathered = (
        lax.all_gather(left_projection, ("branch", "chan"), axis=0, tiled=True),
        lax.all_gather(right_projection, ("branch", "chan"), axis=0, tiled=True),
    )
    column_index = lax.axis_index("branch") * lax.axis_size("chan") + lax.axis_index("chan")
    right_block = lax.dynamic_slice_in_dim(
        right_gathered,
        column_index * (column_block * outer_factor_width),
        column_block * outer_factor_width,
        1,
    )
    left_block = lax.all_to_all(left_gathered, "dap", split_axis=1, concat_axis=0, tiled=True)
    right_full = lax.all_gather(right_block, "dap", axis=0, tiled=True)
    total_seqs = left_block.shape[0]
    outer = jnp.einsum(
        "sic,sjd->ijcd",
        left_block.reshape(total_seqs, rows_block, outer_factor_width),
        right_full.reshape(total_seqs, column_block, outer_factor_width),
        preferred_element_type=jnp.float32,
    ) * (1.0 / total_seqs)
    flat_outer = outer.astype(jnp.bfloat16).reshape(
        rows_block * column_block, outer_factor_width * outer_factor_width
    )
    outer_update = jnp.dot(
        flat_outer, outer_output_weight, preferred_element_type=jnp.float32
    ).reshape(rows_block, column_block, pair_width)
    pair_activation_output = (
        pair_activation_input.astype(jnp.float32) + tri_update + outer_update
    ).astype(jnp.bfloat16)
    return (alignment_output, pair_activation_output)


LANES = 128
SUB = 8


def dot_nn(left, right):
    return lax.dot_general(left, right, (((1,), (0,)), ((), ())), preferred_element_type=jnp.float32)


def dot_nt(left, right):
    return lax.dot_general(left, right, (((1,), (1,)), ((), ())), preferred_element_type=jnp.float32)


def chunk_swap(parts, width):
    parts = list(parts)
    lane = lax.broadcasted_iota(jnp.int32, parts[0].shape, parts[0].ndim - 1)
    axis = parts[0].ndim - 1
    step = len(parts) // 2
    while step >= 1:
        span = step * width
        low = (lane // span) % 2 == 0
        for a in range(len(parts)):
            if (a // step) % 2 == 0:
                lo, hi = parts[a], parts[a + step]
                parts[a] = jnp.where(low, lo, pltpu.roll(hi, span, axis))
                parts[a + step] = jnp.where(low, pltpu.roll(lo, LANES - span, axis), hi)
        step //= 2
    return parts


def norm_rows(values, gain):
    center = values - jnp.mean(values, axis=-1, keepdims=True)
    spread = jnp.mean(center * center, axis=-1, keepdims=True)
    return center * lax.rsqrt(spread + 1e-05) * gain


def staged_kernel(sizes, order, *refs):
    count = len(order)
    sources, rest = refs[:count], refs[count : len(refs) - count - 1]
    held, sems = refs[len(refs) - count - 1 : -1], refs[-1]
    fetches = [pltpu.make_async_copy(sources[i], held[i], sems.at[i]) for i in range(count)]

    def begin():
        for i in order:
            fetches[i].start()

    def ready(*which):
        for i in which:
            fetches[i].wait()

    block_kernel(sizes, begin, ready, *held, *rest)


def block_kernel(
    sizes,
    begin,
    ready,
    feat,
    tokens,
    amask,
    pair,
    pmask,
    table,
    focus_gain,
    entry,
    exit_w,
    pair_gain,
    head_t,
    product_gain,
    prod_t,
    outer_w,
    tri_w,
    tri_gain,
    tri_out,
    align_out,
    pair_out,
    pn,
    bsend,
    brecv,
    tsend,
    trecv,
    lsend,
    rsend,
    lrecv,
    rrecv,
    zsend,
    zrecv,
    stage_a,
    stage_b,
    bias_full,
    emb,
    qm,
    kv,
    gates,
    normed,
    w2t,
    upd,
    rblk,
    obuf,
    table_f,
    left_w,
    gate_f,
    b_send,
    b_recv,
    t_send,
    t_recv,
    o_send,
    o_recv,
    z_send,
    z_recv,
    l_send,
    l_recv,
):
    P_, B_, K_ = sizes
    Q_ = B_ * K_
    D_ = P_ * Q_
    rows, cols, cz = pair.shape
    seqs, res, width = feat.shape
    heads = head_t.shape[0]
    hw = width // heads
    per = LANES // hw
    groups = width // LANES
    fac = prod_t.shape[0] // 2
    nch = LANES // cols
    G = rows // nch
    mp = lax.axis_index("dap")
    mb = lax.axis_index("branch")
    mk = lax.axis_index("chan")
    mq = mb * K_ + mk
    me = mp * Q_ + mq

    def peer(off):
        dp, db, dk = off // Q_, (off // K_) % B_, off % K_
        p, b, k = mp ^ dp, mb ^ db, mk ^ dk
        return p, b * K_ + k, {"dap": p, "branch": b, "chan": k}

    def remote(src, dst, ss, rs, dev):
        return pltpu.make_async_remote_copy(
            src_ref=src,
            dst_ref=dst,
            send_sem=ss,
            recv_sem=rs,
            device_id=dev,
            device_id_type=pl.DeviceIdType.MESH,
        )

    def exchange(send, recv, ss, rs, offs):
        copies = []
        for off in offs:
            p, q, dev = peer(off)
            c = remote(send(p, q), recv.at[me], ss.at[off], rs.at[off], dev)
            c.start()
            copies.append(c)
        return copies

    def forward(copies, recv, ss, rs):
        for op in range(1, P_):
            copies[op - 1].wait_recv()
            src = (mp ^ op) * Q_ + mq
            for oq in range(1, Q_):
                c = remote(
                    recv.at[src], recv.at[src], ss.at[op * Q_ + oq], rs.at[op * Q_ + oq], peer(oq)[2]
                )
                c.start()
                copies.append(c)

    z_offs = [op * Q_ for op in range(1, P_)]
    q_offs = list(range(1, Q_))
    all_offs = sorted(range(1, D_), key=lambda off: (-(off // Q_), off % Q_))
    near_offs = [off for off in all_offs if (off // K_) % B_ == 0]
    cross_offs = [off for off in all_offs if (off // K_) % B_ == 1]

    begin()
    barrier = pltpu.get_barrier_semaphore()
    for off in range(1, D_):
        pl.semaphore_signal(
            barrier, inc=1, device_id=peer(off)[2], device_id_type=pl.DeviceIdType.MESH
        )

    ready(3, 9)
    pair_f = pair[...].astype(jnp.float32).reshape(rows * cols, cz)
    pn[...] = norm_rows(pair_f, pair_gain[...]).astype(jnp.bfloat16)

    def pair_rows(g):
        return jnp.concatenate(
            [pn[(a * G + g) * cols : (a * G + g + 1) * cols, :] for a in range(nch)], axis=0
        )

    ready(10)
    for g in range(G):
        bsend[g * heads : (g + 1) * heads, :] = dot_nt(head_t[...], pair_rows(g))
    brecv[me] = bsend[...]
    pl.semaphore_wait(barrier, D_ - 1)
    bias_z = exchange(lambda p, q: bsend, brecv, b_send, b_recv, z_offs)
    xoff = K_

    def pass_on(src, slot, index, off):
        c = remote(src, brecv.at[slot], b_send.at[index], b_recv.at[index], peer(off)[2])
        c.start()
        return c

    bias_x = [pass_on(bsend, me, Q_ * P_, xoff)]
    bias_c = [pass_on(bsend, me, Q_ * P_ + P_, 1)]

    per_dev = cz // D_
    unit = G * per_dev
    ready(4, 14)
    mrows = jnp.concatenate(
        [pmask[a * G : (a + 1) * G, :].astype(jnp.float32) for a in range(nch)], axis=1
    )
    tri_copies = []
    for side in range(2):
        at = 2 * side * cz
        tri_t = tri_w[:, at : at + 2 * cz].astype(jnp.float32).T.astype(jnp.bfloat16)
        for t in range(G // 2):
            block = jnp.concatenate([pair_rows(2 * t), pair_rows(2 * t + 1)], axis=0)
            lin = dot_nt(tri_t, block)
            mrow = jnp.concatenate([mrows[2 * t : 2 * t + 1], mrows[2 * t + 1 : 2 * t + 2]], axis=1)
            val = jax.nn.sigmoid(lin[cz:]) * lin[:cz] * mrow
            for n in range(D_):
                piece = val[n * per_dev : (n + 1) * per_dev]
                two = jnp.concatenate([piece[:, :LANES], piece[:, LANES:]], axis=0)
                tsend[side, n, 2 * t * per_dev : 2 * (t + 1) * per_dev, :] = two.astype(
                    jnp.bfloat16
                )
        trecv[side, me] = tsend[side, me]
        tri_copies.append(
            exchange(
                lambda p, q: tsend.at[side, p * Q_ + q],
                trecv.at[side],
                t_send.at[side],
                t_recv.at[side],
                near_offs,
            )
        )

    for op in range(1, P_):
        bias_z[op - 1].wait_recv()
        slot = (mp ^ op) * Q_ + mq
        bias_x.append(pass_on(brecv.at[slot], slot, Q_ * P_ + op, xoff))
        bias_c.append(pass_on(brecv.at[slot], slot, Q_ * P_ + P_ + op, 1))
    for side in range(2):
        tri_copies[side] += exchange(
            lambda p, q: tsend.at[side, p * Q_ + q],
            trecv.at[side],
            t_send.at[side],
            t_recv.at[side],
            cross_offs,
        )

    ready(0, 1, 2, 5, 6, 7, 8, 11, 12, 13, 15, 16)
    table_f[...] = jnp.zeros_like(table_f)
    table_f[: table.shape[0], :] = table[...].astype(jnp.float32)
    table_all = table_f[...].astype(jnp.bfloat16)
    four = jnp.concatenate([prod_t[:fac, :].astype(jnp.float32)] * nch, axis=0).T
    lane_fac = lax.broadcasted_iota(jnp.int32, four.shape, 1) // fac
    for a in range(nch):
        left_w[a * width : (a + 1) * width, :] = jnp.where(lane_fac == a, four, 0.0).astype(
            jnp.bfloat16
        )
    lane_head = lax.broadcasted_iota(jnp.int32, (res, LANES), 1) // hw
    for s in range(seqs):
        kinds = lax.broadcasted_iota(jnp.int32, (LANES, res), 0)
        hot = jnp.where(kinds == tokens[s : s + 1, :], 1.0, 0.0).astype(jnp.float32)
        here = feat[s].astype(jnp.float32) + dot_nn(hot.T.astype(jnp.bfloat16), table_all)
        emb[s] = here
        proj = dot_nn(norm_rows(here, focus_gain[...]).astype(jnp.bfloat16), entry[...])
        for b in range(groups):
            qb = proj[:, b * LANES : (b + 1) * LANES]
            for h in range(per):
                qm[s, b, h * res : (h + 1) * res, :] = jnp.where(
                    lane_head == h, qb, 0.0
                ).astype(jnp.bfloat16)
        kv[s] = proj[:, width : 3 * width].astype(jnp.bfloat16)
        gates[s] = jax.nn.sigmoid(proj[:, 3 * width :])

    stage_a[...] = outer_w[...].astype(jnp.float32)
    for g in range(SUB):
        piece = jnp.concatenate(
            [stage_a[pl.ds(a * SUB + g, fac, stride=fac), :] for a in range(fac // SUB)], axis=0
        )
        w2t[:, g * LANES : (g + 1) * LANES] = piece.T.astype(jnp.bfloat16)

    for op in range(P_):
        bias_x[op].wait_recv()
        slot = (mp ^ op) * Q_ + (mb ^ 1) * K_ + mk
        bias_c.append(pass_on(brecv.at[slot], slot, Q_ * P_ + 2 * P_ + op, 1))
    for c in bias_c:
        c.wait_recv()
    for p in range(P_):
        got = chunk_swap([brecv[p * Q_ + q] for q in range(Q_)], cols)
        for a in range(nch):
            stage_a[(p * nch + a) * G * heads : (p * nch + a + 1) * G * heads, :] = got[a]
    for h in range(heads):
        bias_full[h * res : (h + 1) * res, :] = stage_a[pl.ds(h, res, stride=heads), :]

    scale = hw ** (-0.5)
    for s in range(seqs):
        mask_row = (amask[s : s + 1, :].astype(jnp.float32) - 1.0) * 1000000000.0
        gated = []
        for b in range(groups):
            key = kv[s, :, b * LANES : (b + 1) * LANES]
            val = kv[s, :, width + b * LANES : width + (b + 1) * LANES]
            sc = dot_nt(qm[s, b], key) * scale
            sc = sc + bias_full[b * per * res : (b + 1) * per * res, :] + mask_row
            ex = jnp.exp(sc - jnp.max(sc, axis=1, keepdims=True))
            wt = (ex / jnp.sum(ex, axis=1, keepdims=True)).astype(jnp.bfloat16)
            av = dot_nn(wt, val)
            att = av[:res]
            for h in range(1, per):
                att = jnp.where(lane_head == h, av[h * res : (h + 1) * res], att)
            gated.append((att * gates[s, :, b * LANES : (b + 1) * LANES]).astype(jnp.bfloat16))
        out = (emb[s] + dot_nn(jnp.concatenate(gated, axis=1), exit_w[...])).astype(jnp.bfloat16)
        align_out[s] = out
        on = norm_rows(out.astype(jnp.float32), product_gain[...])
        on = on.astype(jnp.bfloat16).astype(jnp.float32)
        mcol = jnp.broadcast_to(amask[s : s + 1, :].astype(jnp.float32), (res, res)).T
        for b in range(groups):
            normed[b, s * res : (s + 1) * res, :] = on[:, b * LANES : (b + 1) * LANES] * mcol

    each = seqs * res // nch
    wide = [
        normed[b, pl.ds(a, each, stride=nch), :].astype(jnp.bfloat16)
        for a in range(nch)
        for b in range(groups)
    ]
    left = dot_nn(jnp.concatenate(wide, axis=1), left_w[...])
    rows_all = jnp.concatenate([normed[b] for b in range(groups)], axis=1).astype(jnp.bfloat16)
    right = dot_nt(prod_t[fac:, :], rows_all)
    lefts = [
        jnp.concatenate(
            [left[(s * P_ + p) * G : (s * P_ + p + 1) * G] for s in range(seqs)], axis=0
        ).astype(jnp.bfloat16)
        for p in range(P_)
    ]
    by_seq = []
    for s in range(seqs):
        by_seq.append(
            chunk_swap(
                [right[a * SUB : (a + 1) * SUB, s * res : (s + 1) * res] for a in range(nch)], cols
            )
        )
    half = seqs * SUB
    for p in range(P_):
        lsend[p] = lefts[p]
    for q in range(Q_):
        rsend[q] = jnp.concatenate([by_seq[s][q] for s in range(seqs)], axis=0).astype(jnp.bfloat16)
    lrecv[me] = lsend[mp]
    rrecv[me] = rsend[mq]
    left_copies = exchange(lambda p, q: lsend.at[p], lrecv, l_send, l_recv, z_offs + q_offs)
    right_copies = exchange(lambda p, q: rsend.at[q], rrecv, o_send, o_recv, all_offs)

    for g in range(G):
        gate_f[g] = jax.nn.sigmoid(dot_nn(pair_rows(g), tri_w[:, 4 * cz :]))

    for side, stage in enumerate((stage_a, stage_b)):
        for c in tri_copies[side]:
            c.wait_recv()
        for p in range(P_):
            got = chunk_swap(
                [
                    trecv[side, p * Q_ + q].astype(jnp.float32)
                    for q in range(Q_)
                ],
                cols,
            )
            for a in range(nch):
                stage[(p * nch + a) * unit : (p * nch + a + 1) * unit, :] = got[a]
    sums = []
    for c in range(per_dev):
        lc = stage_a[pl.ds(c, res, stride=per_dev), :].astype(jnp.bfloat16)
        rc = stage_b[pl.ds(c, res, stride=per_dev), :].astype(jnp.bfloat16)
        sums.append(dot_nt(lc, rc))
    forward(left_copies, lrecv, l_send, l_recv)
    for c in range(per_dev):
        z = sums[c]
        for p in range(P_):
            got = chunk_swap(
                [z[(p * nch + a) * G : (p * nch + a + 1) * G] for a in range(nch)], cols
            )
            for q in range(Q_):
                stage_a[pl.ds((p * Q_ + q) * unit + c, G, stride=per_dev), :] = got[q]
    for n in range(D_):
        zsend[n] = stage_a[n * unit : (n + 1) * unit, :].astype(jnp.bfloat16)
    zrecv[me] = zsend[me]
    sum_copies = exchange(lambda p, q: zsend.at[p * Q_ + q], zrecv, z_send, z_recv, all_offs)

    for c in left_copies[P_ - 1 :] + right_copies:
        c.wait_recv()
    total = D_ * half
    for n in range(D_):
        stage_a[n * half : (n + 1) * half, :] = lrecv[n].astype(jnp.float32)
        stage_b[n * half : (n + 1) * half, :] = rrecv[n].astype(jnp.float32)
    seq_all = D_ * seqs
    gh = G // nch
    lhs = jnp.concatenate(
        [
            jnp.concatenate(
                [stage_a[pl.ds(a * gh + h, seq_all, stride=SUB), :] for a in range(nch)], axis=0
            ).T
            for h in range(gh)
        ],
        axis=0,
    ).astype(jnp.bfloat16)
    lane_col = lax.broadcasted_iota(jnp.int32, (seq_all, LANES), 1) // cols
    keep = [jnp.where(lane_col == a, 1.0, 0.0).astype(jnp.bfloat16) for a in range(nch)]
    for k in range(SUB):
        here = stage_b[pl.ds(k, seq_all, stride=SUB), :]
        turned = [here] + [pltpu.roll(here, r * cols, 1) for r in range(1, nch)]
        turned = [x.astype(jnp.bfloat16) for x in turned]
        for d in range(nch):
            at = (k * nch + d) * LANES
            for a in range(nch):
                rblk[a * seq_all : (a + 1) * seq_all, at : at + LANES] = (
                    turned[(a - d) % nch] * keep[a]
                )
    for t in range(fac // 2):
        prod = dot_nn(lhs, rblk[:, 2 * t * LANES : 2 * (t + 1) * LANES]).astype(jnp.bfloat16)
        for g in range(G):
            for e in range(2):
                obuf[g // 2, (2 * t + e) * fac : (2 * t + e + 1) * fac, (g % 2) * LANES : (g % 2 + 1) * LANES] = prod[
                    g * fac : (g + 1) * fac, e * LANES : (e + 1) * LANES
                ]
    for t in range(G // 2):
        both = dot_nn(w2t[...], obuf[t]) * (1.0 / seq_all)
        for e in range(2):
            g = 2 * t + e
            up = both[:, e * LANES : (e + 1) * LANES].T
            for a in range(nch):
                sl = slice(a * cols, (a + 1) * cols)
                upd[g, sl, :] = pair[a * G + g].astype(jnp.float32) + up[sl]

    for c in sum_copies:
        c.wait_recv()
    for n in range(D_):
        stage_a[n * unit : (n + 1) * unit, :] = zrecv[n].astype(jnp.float32)
    for g in range(G):
        sums_g = jnp.concatenate(
            [stage_a[n * unit + g * per_dev : n * unit + (g + 1) * per_dev, :] for n in range(D_)],
            axis=0,
        ).T
        tn = norm_rows(sums_g, tri_gain[...]).astype(jnp.bfloat16)
        both = upd[g] + gate_f[g] * dot_nn(tn, tri_out[...])
        for a in range(nch):
            i = a * G + g
            sl = slice(a * cols, (a + 1) * cols)
            pair_out[i] = both[sl].astype(jnp.bfloat16)
    for c in bias_z + bias_x + bias_c + tri_copies[0] + tri_copies[1]:
        c.wait_send()
    for c in left_copies + right_copies + sum_copies:
        c.wait_send()


def settle_kernel(one, two, one_out, two_out, one_held, two_held, sems):
    come = [
        pltpu.make_async_copy(one, one_held, sems.at[0]),
        pltpu.make_async_copy(two, two_held, sems.at[1]),
    ]
    go = [
        pltpu.make_async_copy(one_held, one_out, sems.at[2]),
        pltpu.make_async_copy(two_held, two_out, sems.at[3]),
    ]
    for c in come:
        c.start()
    for c, d in zip(come, go):
        c.wait()
        d.start()
    for d in go:
        d.wait()


def kernel_fits(P_, B_, K_, args):
    Q_ = B_ * K_
    feat, pair, head_w, prod_w = args[0], args[3], args[10], args[12]
    rows, cols, cz = pair.shape
    seqs, res, width = feat.shape
    heads = head_w.shape[1]
    fac = prod_w.shape[1] // 2
    nch = LANES // cols
    return (
        res == LANES
        and cz == LANES
        and rows == cols
        and fac == cols
        and nch == P_
        and nch == Q_
        and rows == nch * SUB
        and cz == P_ * Q_ * SUB
        and heads == SUB
        and width % LANES == 0
        and LANES % (width // heads) == 0
        and D_rows(P_, Q_, seqs) <= fac * fac
        and B_ == 2
        and K_ == 2
    )


def D_rows(P_, Q_, seqs):
    return P_ * Q_ * seqs * SUB


def fused(*args):
    P_ = lax.axis_size("dap")
    B_ = lax.axis_size("branch")
    K_ = lax.axis_size("chan")
    Q_ = B_ * K_
    D_ = P_ * Q_
    if not kernel_fits(P_, B_, K_, args):
        return shards(*args)
    (feat, tokens, amask, pair, pmask, table, focus_gain, entry, exit_w, pair_gain, head_w) = args[:11]
    (product_gain, prod_w, outer_w, tri_w, tri_gain, tri_out) = args[11:]
    rows, cols, cz = pair.shape
    seqs, res, width = feat.shape
    heads = head_w.shape[1]
    fac = prod_w.shape[1] // 2
    nch = LANES // cols
    G = rows // nch
    per = LANES // (width // heads)
    operands = (
        feat,
        tokens,
        amask,
        pair,
        pmask,
        table,
        focus_gain[None, :],
        entry,
        exit_w,
        pair_gain[None, :],
        head_w.T,
        product_gain[None, :],
        prod_w.T,
        outer_w,
        tri_w,
        tri_gain[None, :],
        tri_out,
    )
    order = (3, 9, 10, 14, 4, 0, 1, 5, 6, 7, 13, 12, 2, 8, 11, 15, 16)
    per_dev = cz // D_
    unit = G * per_dev
    half = seqs * SUB
    seq_all = D_ * seqs
    f32, bf16 = jnp.float32, jnp.bfloat16
    vm = pltpu.VMEM
    dma = pltpu.SemaphoreType.DMA
    results = pl.pallas_call(
        functools.partial(staged_kernel, (P_, B_, K_), order),
        out_shape=(
            jax.ShapeDtypeStruct(feat.shape, bf16),
            jax.ShapeDtypeStruct(pair.shape, bf16),
        ),
        in_specs=[pl.BlockSpec(memory_space=pltpu.HBM)] * len(operands),
        out_specs=(pl.BlockSpec(memory_space=vm), pl.BlockSpec(memory_space=vm)),
        scratch_shapes=[
            vm((rows * cols, cz), bf16),
            vm((G * heads, LANES), f32),
            vm((D_, G * heads, LANES), f32),
            vm((2, D_, unit, LANES), bf16),
            vm((2, D_, unit, LANES), bf16),
            vm((P_, half, LANES), bf16),
            vm((Q_, half, LANES), bf16),
            vm((D_, half, LANES), bf16),
            vm((D_, half, LANES), bf16),
            vm((D_, unit, LANES), bf16),
            vm((D_, unit, LANES), bf16),
            vm((fac * fac, LANES), f32),
            vm((fac * fac, LANES), f32),
            vm((heads * res, LANES), f32),
            vm((seqs, res, width), f32),
            vm((seqs, width // LANES, per * res, LANES), bf16),
            vm((seqs, res, 2 * width), bf16),
            vm((seqs, res, width), f32),
            vm((width // LANES, seqs * res, LANES), f32),
            vm((cz, fac * fac), bf16),
            vm((G, LANES, LANES), f32),
            vm((nch * seq_all, fac * LANES), bf16),
            vm((G // 2, fac * fac, 2 * LANES), bf16),
            vm((LANES, width), f32),
            vm((nch * width, nch * fac), bf16),
            vm((G, LANES, cz), f32),
            dma((Q_ * P_ + 3 * P_,)),
            dma((Q_ * P_ + 3 * P_,)),
            dma((2, D_)),
            dma((2, D_)),
            dma((D_,)),
            dma((D_,)),
            dma((D_,)),
            dma((D_,)),
            dma((D_,)),
            dma((D_,)),
        ]
        + [vm(x.shape, x.dtype) for x in operands]
        + [dma((len(operands),))],
        compiler_params=pltpu.CompilerParams(collective_id=0, has_side_effects=True),
    )(*operands)
    return pl.pallas_call(
        settle_kernel,
        out_shape=tuple(jax.ShapeDtypeStruct(x.shape, x.dtype) for x in results),
        in_specs=[pl.BlockSpec(memory_space=pltpu.HBM)] * 2,
        out_specs=(pl.BlockSpec(memory_space=pltpu.HBM),) * 2,
        scratch_shapes=[vm(x.shape, x.dtype) for x in results] + [dma((4,))],
    )(*results)


def solution(mesh):
    in_specs = (
        P(("groups", "dap", "branch", "chan"), None, None),
        P(("groups", "dap", "branch", "chan"), None),
        P(("groups", "dap", "branch", "chan"), None),
        P(("groups", "dap"), ("branch", "chan"), None),
        P(("groups", "dap"), ("branch", "chan")),
        P(),
        P(),
        P(),
        P(),
        P(),
        P(),
        P(),
        P(),
        P(),
        P(),
        P(),
        P(),
    )
    out_specs = (
        P(("groups", "dap", "branch", "chan"), None, None),
        P(("groups", "dap"), ("branch", "chan"), None),
    )
    return jax.shard_map(fused, mesh=mesh, in_specs=in_specs, out_specs=out_specs, check_vma=False)
```

```python
import functools

import jax
import jax.numpy as jnp
from jax import lax
from jax.experimental import pallas as pl
from jax.experimental.pallas import tpu as pltpu
from jax.sharding import PartitionSpec as P


def layer_normalize(values, gain_vector, norm_axis):
    center = values - jnp.mean(values, axis=norm_axis, keepdims=True)
    spread = jnp.mean(center * center, axis=norm_axis, keepdims=True)
    return center * lax.rsqrt(spread + 1e-05) * gain_vector


def channel_products(left_part, right_part, dap_count, column_count, rows_block, column_block):
    row_ratio = dap_count // column_count
    channels_here = left_part.size // (dap_count * column_count * rows_block * column_block)
    left_five = left_part.reshape(dap_count, column_count, channels_here, rows_block, column_block)
    right_six = right_part.reshape(
        column_count, row_ratio, column_count, channels_here, rows_block, column_block
    )
    product = jnp.einsum(
        "pqrik,bhqrjk->pbrihj", left_five, right_six, preferred_element_type=jnp.float32
    )
    return product.astype(jnp.bfloat16)


def shards(
    homolog_features,
    alignment_tokens,
    alignment_mask,
    pair_activation_input,
    pair_residue_mask,
    letter_lookup_matrix,
    homolog_focus_scaling,
    focus_entry_matrix,
    focus_exit_matrix,
    pair_norm_gain,
    head_bias_weight,
    tensor_product_scaling,
    tensor_product_matrix,
    outer_output_weight,
    triangle_input_weight,
    triangle_norm_gain,
    triangle_output_weight,
):
    dap_count = lax.axis_size("dap")
    column_count = lax.axis_size("branch") * lax.axis_size("chan")
    device_count = dap_count * column_count
    rows_block, column_block, pair_width = pair_activation_input.shape
    sequence_total, residue_total, alignment_width = homolog_features.shape
    number_heads = head_bias_weight.shape[1]
    per_head_width = alignment_width // number_heads
    outer_factor_width = tensor_product_matrix.shape[1] // 2
    pair_normed = layer_normalize(
        pair_activation_input.astype(jnp.float32), pair_norm_gain, -1
    ).astype(jnp.bfloat16)
    bias_block = jnp.einsum(
        "ikc,ch->hik", pair_normed, head_bias_weight, preferred_element_type=jnp.float32
    )
    tri_linear = jnp.einsum(
        "ikc,ce->eik",
        pair_normed,
        triangle_input_weight[:, : 4 * pair_width],
        preferred_element_type=jnp.float32,
    )
    mask_pair = pair_residue_mask.astype(jnp.float32)
    tri_left = (
        jax.nn.sigmoid(tri_linear[pair_width : 2 * pair_width])
        * tri_linear[:pair_width]
        * mask_pair
    ).astype(jnp.bfloat16)
    tri_right = (
        jax.nn.sigmoid(tri_linear[3 * pair_width : 4 * pair_width])
        * tri_linear[2 * pair_width : 3 * pair_width]
        * mask_pair
    ).astype(jnp.bfloat16)
    out_gate = jnp.einsum(
        "ikc,ce->ike",
        pair_normed,
        triangle_input_weight[:, 4 * pair_width :],
        preferred_element_type=jnp.float32,
    )
    per_device = pair_width // device_count
    flat_shape = (device_count, 1, per_device, rows_block, column_block)
    products = channel_products(
        lax.all_to_all(
            tri_left.reshape(flat_shape),
            ("dap", "branch", "chan"),
            split_axis=0,
            concat_axis=1,
            tiled=True,
        ),
        lax.all_to_all(
            tri_right.reshape(flat_shape),
            ("dap", "branch", "chan"),
            split_axis=0,
            concat_axis=1,
            tiled=True,
        ),
        dap_count,
        column_count,
        rows_block,
        column_block,
    )
    channels_here = products.shape[2]
    sending = products.reshape(device_count, 1, channels_here, rows_block, column_block)
    returned = lax.all_to_all(
        sending, ("dap", "branch", "chan"), split_axis=0, concat_axis=1, tiled=True
    )
    tri_sum = returned.reshape(pair_width, rows_block, column_block)
    tri_normed = layer_normalize(
        tri_sum.astype(jnp.float32), triangle_norm_gain[:, None, None], 0
    ).astype(jnp.bfloat16)
    tri_update = jax.nn.sigmoid(out_gate) * jnp.einsum(
        "cik,ce->ike", tri_normed, triangle_output_weight, preferred_element_type=jnp.float32
    )
    token_class_count = letter_lookup_matrix.shape[0]
    token_indicator = (
        alignment_tokens[:, :, None] == jnp.arange(token_class_count, dtype=jnp.int32)
    ).astype(jnp.bfloat16)
    embedded_tokens = homolog_features.astype(jnp.float32) + jnp.einsum(
        "snv,vc->snc", token_indicator, letter_lookup_matrix, preferred_element_type=jnp.float32
    )
    alignment_normalized = layer_normalize(embedded_tokens, homolog_focus_scaling, -1).astype(
        jnp.bfloat16
    )
    projected_values = jnp.einsum(
        "rdz,zg->rdg", alignment_normalized, focus_entry_matrix, preferred_element_type=jnp.float32
    )
    query_rows = projected_values[:, :, :alignment_width].astype(jnp.bfloat16)
    every_key = projected_values[:, :, alignment_width : 2 * alignment_width].astype(jnp.bfloat16)
    every_value = projected_values[:, :, 2 * alignment_width : 3 * alignment_width].astype(
        jnp.bfloat16
    )
    gate_values = projected_values[:, :, 3 * alignment_width :]
    key_mask_bias = (alignment_mask.astype(jnp.float32) - 1.0) * 1000000000.0
    score_scale = per_head_width ** (-0.5)
    bias_partial = lax.all_gather(bias_block, ("branch", "chan"), axis=2, tiled=True)
    bias_full = lax.all_gather(bias_partial, "dap", axis=1, tiled=True)
    query_form = query_rows.reshape(sequence_total, residue_total, number_heads, per_head_width)
    key_form = every_key.reshape(sequence_total, residue_total, number_heads, per_head_width)
    value_form = every_value.reshape(sequence_total, residue_total, number_heads, per_head_width)
    mask_form = key_mask_bias.reshape(sequence_total, 1, 1, residue_total)

    def attend(seq_item):
        query_seq, key_seq, value_seq, mask_seq = seq_item
        scores = (
            jnp.einsum("ihd,jhd->hij", query_seq, key_seq, preferred_element_type=jnp.float32)
            * score_scale
            + bias_full
            + mask_seq
        )
        largest = jnp.max(scores, axis=2, keepdims=True)
        exponent = jnp.exp(scores - largest)
        attention_weights = (exponent / jnp.sum(exponent, axis=2, keepdims=True)).astype(
            jnp.bfloat16
        )
        return jnp.einsum(
            "bqo,obm->qbm", attention_weights, value_seq, preferred_element_type=jnp.float32
        )

    attended_rows = lax.map(attend, (query_form, key_form, value_form, mask_form)).reshape(
        sequence_total, residue_total, alignment_width
    )
    gated_output = (attended_rows * jax.nn.sigmoid(gate_values)).astype(jnp.bfloat16)
    alignment_output = (
        embedded_tokens
        + jnp.einsum(
            "rdz,zg->rdg", gated_output, focus_exit_matrix, preferred_element_type=jnp.float32
        )
    ).astype(jnp.bfloat16)
    outer_normalized = layer_normalize(
        alignment_output.astype(jnp.float32), tensor_product_scaling, -1
    ).astype(jnp.bfloat16)
    alignment_mask_rows = alignment_mask.astype(jnp.float32)[:, :, None]
    left_projection = (
        (
            jnp.einsum(
                "rdz,zg->rdg",
                outer_normalized,
                tensor_product_matrix[:, :outer_factor_width],
                preferred_element_type=jnp.float32,
            )
            * alignment_mask_rows
        )
        .astype(jnp.bfloat16)
        .reshape(sequence_total, residue_total * outer_factor_width)
    )
    right_projection = (
        (
            jnp.einsum(
                "rdz,zg->rdg",
                outer_normalized,
                tensor_product_matrix[:, outer_factor_width:],
                preferred_element_type=jnp.float32,
            )
            * alignment_mask_rows
        )
        .astype(jnp.bfloat16)
        .reshape(sequence_total, residue_total * outer_factor_width)
    )
    left_gathered, right_gathered = (
        lax.all_gather(left_projection, ("branch", "chan"), axis=0, tiled=True),
        lax.all_gather(right_projection, ("branch", "chan"), axis=0, tiled=True),
    )
    column_index = lax.axis_index("branch") * lax.axis_size("chan") + lax.axis_index("chan")
    right_block = lax.dynamic_slice_in_dim(
        right_gathered,
        column_index * (column_block * outer_factor_width),
        column_block * outer_factor_width,
        1,
    )
    left_block = lax.all_to_all(left_gathered, "dap", split_axis=1, concat_axis=0, tiled=True)
    right_full = lax.all_gather(right_block, "dap", axis=0, tiled=True)
    total_seqs = left_block.shape[0]
    outer = jnp.einsum(
        "sic,sjd->ijcd",
        left_block.reshape(total_seqs, rows_block, outer_factor_width),
        right_full.reshape(total_seqs, column_block, outer_factor_width),
        preferred_element_type=jnp.float32,
    ) * (1.0 / total_seqs)
    flat_outer = outer.astype(jnp.bfloat16).reshape(
        rows_block * column_block, outer_factor_width * outer_factor_width
    )
    outer_update = jnp.dot(
        flat_outer, outer_output_weight, preferred_element_type=jnp.float32
    ).reshape(rows_block, column_block, pair_width)
    pair_activation_output = (
        pair_activation_input.astype(jnp.float32) + tri_update + outer_update
    ).astype(jnp.bfloat16)
    return (alignment_output, pair_activation_output)


LANES = 128
SUB = 8
LOG2E = 1.4426950408889634


def dot_nn(left, right):
    return lax.dot_general(left, right, (((1,), (0,)), ((), ())), preferred_element_type=jnp.float32)


def dot_nt(left, right):
    return lax.dot_general(left, right, (((1,), (1,)), ((), ())), preferred_element_type=jnp.float32)


def chunk_swap(parts, width):
    parts = list(parts)
    lane = lax.broadcasted_iota(jnp.int32, parts[0].shape, parts[0].ndim - 1)
    axis = parts[0].ndim - 1
    step = len(parts) // 2
    while step >= 1:
        span = step * width
        low = (lane // span) % 2 == 0
        for a in range(len(parts)):
            if (a // step) % 2 == 0:
                lo, hi = parts[a], parts[a + step]
                parts[a] = jnp.where(low, lo, pltpu.roll(hi, span, axis))
                parts[a + step] = jnp.where(low, pltpu.roll(lo, LANES - span, axis), hi)
        step //= 2
    return parts


def norm_rows(values, gain):
    center = values - jnp.mean(values, axis=-1, keepdims=True)
    spread = jnp.mean(center * center, axis=-1, keepdims=True)
    return center * lax.rsqrt(spread + 1e-05) * gain


def half_sigmoid(values):
    return 0.5 * jnp.tanh(0.5 * values) + 0.5


def wide_stat(parts, ones, width):
    total = sum(dot_nn(x, ones) for x in parts) * (1.0 / width)
    return jnp.concatenate([total] * (width // LANES), axis=1)


def norm_mxu(values, parts, gain, ones):
    width = values.shape[1]
    center = values - wide_stat(parts, ones, width)
    spread = wide_stat([(center * center).astype(jnp.bfloat16)], ones, width)
    return center * lax.rsqrt(spread + 1e-05) * gain


def staged_kernel(sizes, order, *refs):
    count = len(order)
    sources, rest = refs[:count], refs[count : len(refs) - count - 1]
    held, sems = refs[len(refs) - count - 1 : -1], refs[-1]
    fetches = [pltpu.make_async_copy(sources[i], held[i], sems.at[i]) for i in range(count)]

    def begin():
        for i in order:
            fetches[i].start()

    def ready(*which):
        for i in which:
            fetches[i].wait()

    block_kernel(sizes, begin, ready, *held, *rest)


def block_kernel(
    sizes,
    begin,
    ready,
    feat,
    tokens,
    amask,
    pair,
    pmask,
    table,
    focus_gain,
    entry,
    exit_w,
    pair_gain,
    head_t,
    product_gain,
    prod_t,
    outer_w,
    tri_w,
    tri_gain,
    tri_out,
    align_out,
    pair_out,
    pn,
    bsend,
    brecv,
    tsend,
    trecv_l,
    trecv_r,
    lsend,
    rsend,
    lrecv,
    rrecv,
    zsend,
    zrecv,
    stage_a,
    stage_b,
    bias_full,
    emb,
    qd,
    keys,
    entry_t,
    vt,
    rows_n,
    att_t,
    mask_c,
    gates,
    normed,
    w2t,
    upd,
    rblk,
    obuf,
    table_f,
    left_w,
    gate_f,
    b_send,
    b_z,
    b_x,
    b_c,
    t_send,
    t_recv,
    o_send,
    o_recv,
    z_send,
    z_recv,
    l_send,
    l_z,
    l_recv,
):
    P_, B_, K_ = sizes
    Q_ = B_ * K_
    D_ = P_ * Q_
    rows, cols, cz = pair.shape
    seqs, res, width = feat.shape
    heads = head_t.shape[0]
    hw = width // heads
    per = LANES // hw
    groups = width // LANES
    fac = prod_t.shape[0] // 2
    nch = LANES // cols
    G = rows // nch
    mp = lax.axis_index("dap")
    mb = lax.axis_index("branch")
    mk = lax.axis_index("chan")
    mq = mb * K_ + mk
    me = mp * Q_ + mq

    def peer(off):
        dp, db, dk = off // Q_, (off // K_) % B_, off % K_
        p, b, k = mp ^ dp, mb ^ db, mk ^ dk
        return p, b * K_ + k, {"dap": p, "branch": b, "chan": k}

    def remote(src, dst, ss, rs, dev):
        return pltpu.make_async_remote_copy(
            src_ref=src,
            dst_ref=dst,
            send_sem=ss,
            recv_sem=rs,
            device_id=dev,
            device_id_type=pl.DeviceIdType.MESH,
        )

    here_dev = peer(1)[2]

    def sent(ref, sem):
        remote(ref, ref, sem, sem, here_dev).wait_send()

    def arrived(ref, sem):
        remote(ref, ref, sem, sem, here_dev).wait_recv()

    def exchange(send, recv, ss, rs, offs):
        for off in offs:
            p, q, dev = peer(off)
            remote(send(p, q), recv.at[me], ss, rs, dev).start()

    z_offs = [op * Q_ for op in range(1, P_)]
    q_offs = list(range(1, Q_))
    all_offs = sorted(range(1, D_), key=lambda off: (-(off // Q_), off % Q_))

    begin()
    barrier = pltpu.get_barrier_semaphore()
    for off in range(1, D_):
        pl.semaphore_signal(
            barrier, inc=1, device_id=peer(off)[2], device_id_type=pl.DeviceIdType.MESH
        )

    ready(3, 9)
    pair_h = pair[...].reshape(rows * cols, cz)
    ones_z = jnp.ones((cz, LANES), jnp.bfloat16)
    pn[...] = norm_mxu(pair_h.astype(jnp.float32), [pair_h], pair_gain[...], ones_z).astype(
        jnp.bfloat16
    )

    def pair_rows(g):
        return jnp.concatenate(
            [pn[(a * G + g) * cols : (a * G + g + 1) * cols, :] for a in range(nch)], axis=0
        )

    ready(10)
    for g in range(G):
        stage_b[g * heads : (g + 1) * heads, :] = dot_nt(head_t[...], pair_rows(g)) * LOG2E
    for b in range(groups):
        pieces = []
        for h in range(per):
            by_head = stage_b[pl.ds(b * per + h, G, stride=heads), :]
            for a in range(nch):
                pieces.append(pltpu.roll(by_head, LANES - a * cols, 1) if a else by_head)
        bsend[b * cols : (b + 1) * cols, :] = jnp.concatenate(pieces, axis=0).T[:cols]
    brecv[me] = bsend[...]
    pl.semaphore_wait(barrier, D_ - 1)
    for op in range(1, P_):
        p, q, dev = peer(op * Q_)
        remote(bsend, brecv.at[me], b_send, b_z.at[op], dev).start()
    xoff = K_

    def pass_on(src, slot, sem, off):
        remote(src, brecv.at[slot], b_send, sem, peer(off)[2]).start()

    pass_on(bsend, me, b_x.at[0], xoff)
    pass_on(bsend, me, b_c, 1)
    half_p = P_ // 2
    owners = half_p * Q_
    per_dev = cz // owners
    unit = G * per_dev
    mine = (mp % half_p) * Q_ + mq
    ready(4, 14)
    mrows = jnp.concatenate(
        [pmask[a * G : (a + 1) * G, :].astype(jnp.float32) for a in range(nch)], axis=1
    )
    trecv = (trecv_l, trecv_r)

    def tri_factor(side):
        at = 2 * side * cz
        tri_t = tri_w[:, at : at + 2 * cz].astype(jnp.float32).T.astype(jnp.bfloat16)
        for t in range(G // 2):
            block = jnp.concatenate([pair_rows(2 * t), pair_rows(2 * t + 1)], axis=0)
            lin = dot_nt(tri_t, block)
            mrow = jnp.concatenate([mrows[2 * t : 2 * t + 1], mrows[2 * t + 1 : 2 * t + 2]], axis=1)
            val = half_sigmoid(lin[cz:]) * (lin[:cz] * mrow)
            for n in range(owners):
                piece = val[n * per_dev : (n + 1) * per_dev]
                two = jnp.concatenate([piece[:, :LANES], piece[:, LANES:]], axis=0)
                tsend[side, n, 2 * t * per_dev : 2 * (t + 1) * per_dev, :] = two.astype(
                    jnp.bfloat16
                )
        if side == 0:
            trecv_l[mine] = tsend[side, mine]
        else:
            trecv_r[me] = tsend[side, mine]

    def tri_send(side, offs):
        for off in offs:
            p, q, dev = peer(off)
            slot = mine if side == 0 else me
            remote(
                tsend.at[side, (p % half_p) * Q_ + q],
                trecv[side].at[slot],
                t_send.at[side],
                t_recv.at[side],
                dev,
            ).start()

    in_half = [off for off in range(1, D_) if off // Q_ < half_p]
    far = [off for off in range(1, D_) if off // Q_ >= half_p]
    own_row = [off for off in in_half if off < Q_]
    next_row = [off for off in in_half if off >= Q_]
    same_x = lambda offs: [off for off in offs if (off // K_) % B_ == 0]
    other_x = lambda offs: [off for off in offs if (off // K_) % B_ == 1]
    tri_factor(1)
    tri_send(1, same_x(far))
    tri_factor(0)
    tri_send(1, same_x(in_half) + other_x(own_row))
    tri_send(0, same_x(in_half) + other_x(own_row))

    ready(0, 1, 2, 5, 6, 7, 8, 11, 12, 13, 15, 16)
    table_f[...] = jnp.zeros_like(table_f)
    table_f[: table.shape[0], :] = table[...].astype(jnp.float32)
    table_all = table_f[...].astype(jnp.bfloat16)
    kinds_n = table_f.shape[0]
    ones_m = jnp.ones((width, LANES), jnp.bfloat16)
    scale = hw ** (-0.5) * LOG2E
    for n, at in enumerate((0, 2 * width, 3 * width)):
        part = entry[:, at : at + width].astype(jnp.float32).T
        entry_t[n * width : (n + 1) * width, :] = part.astype(jnp.bfloat16)
    qd[...] = jnp.zeros_like(qd)
    for s in range(seqs):
        for h in range(heads):
            vt[s, h, hw:, :] = jnp.ones((vt.shape[2] - hw, res), jnp.bfloat16)
    kinds = lax.broadcasted_iota(jnp.int32, (kinds_n, res), 0)
    hot = jnp.concatenate(
        [jnp.where(kinds == tokens[s : s + 1, :], 1.0, 0.0) for s in range(seqs)], axis=1
    ).astype(jnp.float32)
    here = feat[...].astype(jnp.float32).reshape(seqs * res, width)
    here = here + dot_nn(hot.T.astype(jnp.bfloat16), table_all)
    emb[...] = here
    high = here.astype(jnp.bfloat16)
    low = (here - high.astype(jnp.float32)).astype(jnp.bfloat16)
    rows_n[...] = norm_mxu(here, [high, low], focus_gain[...], ones_m).astype(jnp.bfloat16)
    keys[...] = dot_nn(rows_n[...], entry[:, width : 2 * width]).astype(jnp.bfloat16)
    for u in range(seqs // 2):
        two = rows_n[2 * u * res : 2 * (u + 1) * res, :]
        for n in range(3):
            turned = dot_nt(entry_t[n * width : (n + 1) * width, :], two)
            for v in range(2):
                s = 2 * u + v
                here = turned[:, v * res : (v + 1) * res]
                if n == 2:
                    gates[s] = half_sigmoid(here)
                    continue
                for h in range(heads):
                    b, e = h // per, h % per
                    part = here[h * hw : (h + 1) * hw]
                    if n == 0:
                        qd[s, b, e * hw : (e + 1) * hw, e * res : (e + 1) * res] = (
                            part * scale
                        ).astype(jnp.bfloat16)
                    else:
                        vt[s, h, :hw, :] = part.astype(jnp.bfloat16)

    for op in range(1, P_):
        arrived(bsend, b_z.at[op])
        slot = (mp ^ op) * Q_ + mq
        pass_on(brecv.at[slot], slot, b_x.at[op], xoff)
        pass_on(brecv.at[slot], slot, b_c, 1)
    tri_send(1, other_x(far))
    tri_send(1, other_x(next_row))
    tri_send(0, other_x(next_row))

    four = jnp.concatenate([prod_t[:fac, :].astype(jnp.float32)] * nch, axis=0).T
    lane_fac = lax.broadcasted_iota(jnp.int32, four.shape, 1) // fac
    for a in range(nch):
        left_w[a * width : (a + 1) * width, :] = jnp.where(lane_fac == a, four, 0.0).astype(
            jnp.bfloat16
        )
    for g in range(G):
        gate_f[g] = half_sigmoid(dot_nn(pair_rows(g), tri_w[:, 4 * cz :]))
    stage_a[...] = outer_w[...].astype(jnp.float32)
    for g in range(SUB):
        piece = jnp.concatenate(
            [stage_a[pl.ds(a * SUB + g, fac, stride=fac), :] for a in range(fac // SUB)], axis=0
        )
        w2t[:, g * LANES : (g + 1) * LANES] = piece.T.astype(jnp.bfloat16)

    for op in range(P_):
        arrived(bsend, b_x.at[op])
        slot = (mp ^ op) * Q_ + (mb ^ 1) * K_ + mk
        pass_on(brecv.at[slot], slot, b_c, 1)
    arrived(brecv.at[: 2 * P_], b_c)
    for q in range(Q_):
        for b in range(groups):
            got = chunk_swap(
                [brecv[p * Q_ + q, b * cols : (b + 1) * cols, :] for p in range(P_)], cols
            )
            for h in range(per):
                bias_full[b, q * cols : (q + 1) * cols, h * res : (h + 1) * res] = got[h]

    for s in range(seqs):
        mcol = jnp.broadcast_to(amask[s : s + 1, :].astype(jnp.float32), (res, res)).T
        mask_add = (mcol - 1.0) * (1000000000.0 * LOG2E)
        for h in range(heads):
            b, e = h // per, h % per
            sl = slice(e * res, (e + 1) * res)
            sc = dot_nn(
                keys[s * res : (s + 1) * res, b * LANES : (b + 1) * LANES], qd[s, b, :, sl]
            )
            sc = (sc + bias_full[b, :, sl]) + mask_add
            ex = jnp.exp2(sc - jnp.max(sc, axis=0, keepdims=True)).astype(jnp.bfloat16)
            av = dot_nn(vt[s, h], ex)
            att_t[h * hw : (h + 1) * hw, s * res : (s + 1) * res] = (
                av[:hw] * (1.0 / av[hw : hw + 1]) * gates[s, h * hw : (h + 1) * hw, :]
            )
        mask_c[s * res : (s + 1) * res, :] = mcol
    attended = att_t[...].T.astype(jnp.bfloat16)
    out = (emb[...] + dot_nn(attended, exit_w[...])).astype(jnp.bfloat16)
    align_out[...] = out.reshape(seqs, res, width)
    on = norm_mxu(out.astype(jnp.float32), [out], product_gain[...], ones_m)
    on = on.astype(jnp.bfloat16).astype(jnp.float32)
    for b in range(groups):
        normed[b] = on[:, b * LANES : (b + 1) * LANES] * mask_c[...]

    each = seqs * res // nch
    wide = [
        normed[b, pl.ds(a, each, stride=nch), :].astype(jnp.bfloat16)
        for a in range(nch)
        for b in range(groups)
    ]
    left = dot_nn(jnp.concatenate(wide, axis=1), left_w[...])
    rows_all = jnp.concatenate([normed[b] for b in range(groups)], axis=1).astype(jnp.bfloat16)
    right = dot_nt(prod_t[fac:, :], rows_all)
    lefts = [
        jnp.concatenate(
            [left[(s * P_ + p) * G : (s * P_ + p + 1) * G] for s in range(seqs)], axis=0
        ).astype(jnp.bfloat16)
        for p in range(P_)
    ]
    by_seq = []
    for s in range(seqs):
        by_seq.append(
            chunk_swap(
                [right[a * SUB : (a + 1) * SUB, s * res : (s + 1) * res] for a in range(nch)], cols
            )
        )
    half = seqs * SUB
    for p in range(P_):
        lsend[p] = lefts[p]
    for q in range(Q_):
        rsend[q] = jnp.concatenate([by_seq[s][q] for s in range(seqs)], axis=0).astype(jnp.bfloat16)
    lrecv[me] = lsend[mp]
    rrecv[me] = rsend[mq]
    for op in range(1, P_):
        p, q, dev = peer(op * Q_)
        remote(lsend.at[p], lrecv.at[me], l_send, l_z.at[op], dev).start()
    exchange(lambda p, q: lsend.at[mp], lrecv, l_send, l_recv, q_offs)
    exchange(lambda p, q: rsend.at[q], rrecv, o_send, o_recv, all_offs)

    for side, stage in enumerate((stage_a, stage_b)):
        arrived(trecv[side].at[: (owners if side == 0 else D_) - 1], t_recv.at[side])
        for p in range(half_p if side == 0 else P_):
            got = chunk_swap(
                [trecv[side][p * Q_ + q].astype(jnp.float32) for q in range(Q_)],
                cols,
            )
            for a in range(nch):
                stage[(p * nch + a) * unit : (p * nch + a + 1) * unit, :] = got[a]
    sums = []
    for c in range(per_dev):
        lc = stage_a[pl.ds(c, half_p * rows, stride=per_dev), :].astype(jnp.bfloat16)
        rc = stage_b[pl.ds(c, res, stride=per_dev), :].astype(jnp.bfloat16)
        sums.append(dot_nt(lc, rc))
    for op in range(1, P_):
        arrived(lsend.at[0], l_z.at[op])
        slot = (mp ^ op) * Q_ + mq
        for off in q_offs:
            remote(lrecv.at[slot], lrecv.at[slot], l_send, l_recv, peer(off)[2]).start()
    for c in range(per_dev):
        z = sums[c]
        for p in range(half_p):
            got = chunk_swap(
                [z[(p * nch + a) * G : (p * nch + a + 1) * G] for a in range(nch)], cols
            )
            for q in range(Q_):
                stage_a[pl.ds((p * Q_ + q) * unit + c, G, stride=per_dev), :] = got[q]
    for n in range(owners):
        zsend[n] = stage_a[n * unit : (n + 1) * unit, :].astype(jnp.bfloat16)
    zrecv[mine] = zsend[mine]
    for off in sorted(in_half, reverse=True):
        p, q, dev = peer(off)
        remote(zsend.at[(p % half_p) * Q_ + q], zrecv.at[mine], z_send, z_recv, dev).start()

    arrived(lrecv.at[: P_ * (Q_ - 1)], l_recv)
    arrived(rrecv.at[: D_ - 1], o_recv)
    total = D_ * half
    for n in range(D_):
        stage_a[n * half : (n + 1) * half, :] = lrecv[n].astype(jnp.float32)
        stage_b[n * half : (n + 1) * half, :] = rrecv[n].astype(jnp.float32)
    seq_all = D_ * seqs
    gh = G // nch
    lhs = jnp.concatenate(
        [
            jnp.concatenate(
                [stage_a[pl.ds(a * gh + h, seq_all, stride=SUB), :] for a in range(nch)], axis=0
            ).T
            for h in range(gh)
        ],
        axis=0,
    ).astype(jnp.bfloat16)
    lane_col = lax.broadcasted_iota(jnp.int32, (seq_all, LANES), 1) // cols
    keep = [jnp.where(lane_col == a, 1.0, 0.0).astype(jnp.bfloat16) for a in range(nch)]
    for k in range(SUB):
        here = stage_b[pl.ds(k, seq_all, stride=SUB), :]
        turned = [here] + [pltpu.roll(here, r * cols, 1) for r in range(1, nch)]
        turned = [x.astype(jnp.bfloat16) for x in turned]
        for d in range(nch):
            at = (k * nch + d) * LANES
            for a in range(nch):
                rblk[a * seq_all : (a + 1) * seq_all, at : at + LANES] = (
                    turned[(a - d) % nch] * keep[a]
                )
    for t in range(fac // 2):
        prod = dot_nn(lhs, rblk[:, 2 * t * LANES : 2 * (t + 1) * LANES]).astype(jnp.bfloat16)
        for g in range(G):
            for e in range(2):
                obuf[g // 2, (2 * t + e) * fac : (2 * t + e + 1) * fac, (g % 2) * LANES : (g % 2 + 1) * LANES] = prod[
                    g * fac : (g + 1) * fac, e * LANES : (e + 1) * LANES
                ]
    for t in range(G // 2):
        both = dot_nn(w2t[...], obuf[t]) * (1.0 / seq_all)
        for e in range(2):
            g = 2 * t + e
            up = both[:, e * LANES : (e + 1) * LANES].T
            for a in range(nch):
                sl = slice(a * cols, (a + 1) * cols)
                upd[g, sl, :] = pair[a * G + g].astype(jnp.float32) + up[sl]

    sent(brecv.at[: D_ - 1], b_send)
    sent(trecv_l.at[: owners - 1], t_send.at[0])
    sent(trecv_r.at[: D_ - 1], t_send.at[1])
    sent(lrecv.at[: D_ - 1], l_send)
    sent(rrecv.at[: D_ - 1], o_send)
    arrived(zrecv.at[: owners - 1], z_recv)
    for n in range(owners):
        stage_a[n * unit : (n + 1) * unit, :] = zrecv[n].astype(jnp.float32)
    for g in range(G):
        sums_g = jnp.concatenate(
            [
                stage_a[n * unit + g * per_dev : n * unit + (g + 1) * per_dev, :]
                for n in range(owners)
            ],
            axis=0,
        ).T
        tn = norm_rows(sums_g, tri_gain[...]).astype(jnp.bfloat16)
        both = upd[g] + gate_f[g] * dot_nn(tn, tri_out[...])
        for a in range(nch):
            i = a * G + g
            sl = slice(a * cols, (a + 1) * cols)
            pair_out[i] = both[sl].astype(jnp.bfloat16)
    sent(zrecv.at[: owners - 1], z_send)


def settle_kernel(one, two, one_out, two_out, one_held, two_held, sems):
    come = [
        pltpu.make_async_copy(one, one_held, sems.at[0]),
        pltpu.make_async_copy(two, two_held, sems.at[1]),
    ]
    go = [
        pltpu.make_async_copy(one_held, one_out, sems.at[2]),
        pltpu.make_async_copy(two_held, two_out, sems.at[3]),
    ]
    for c in come:
        c.start()
    for c, d in zip(come, go):
        c.wait()
        d.start()
    for d in go:
        d.wait()


def kernel_fits(P_, B_, K_, args):
    Q_ = B_ * K_
    feat, pair, head_w, prod_w = args[0], args[3], args[10], args[12]
    rows, cols, cz = pair.shape
    seqs, res, width = feat.shape
    heads = head_w.shape[1]
    fac = prod_w.shape[1] // 2
    nch = LANES // cols
    return (
        res == LANES
        and cz == LANES
        and rows == cols
        and fac == cols
        and nch == P_
        and nch == Q_
        and rows == nch * SUB
        and cz == P_ * Q_ * SUB
        and heads == SUB
        and width % LANES == 0
        and width // heads == cols
        and D_rows(P_, Q_, seqs) <= fac * fac
        and B_ == 2
        and K_ == 2
    )


def D_rows(P_, Q_, seqs):
    return P_ * Q_ * seqs * SUB


def fused(*args):
    P_ = lax.axis_size("dap")
    B_ = lax.axis_size("branch")
    K_ = lax.axis_size("chan")
    Q_ = B_ * K_
    D_ = P_ * Q_
    if not kernel_fits(P_, B_, K_, args):
        return shards(*args)
    (feat, tokens, amask, pair, pmask, table, focus_gain, entry, exit_w, pair_gain, head_w) = args[:11]
    (product_gain, prod_w, outer_w, tri_w, tri_gain, tri_out) = args[11:]
    rows, cols, cz = pair.shape
    seqs, res, width = feat.shape
    heads = head_w.shape[1]
    fac = prod_w.shape[1] // 2
    nch = LANES // cols
    G = rows // nch
    per = LANES // (width // heads)
    operands = (
        feat,
        tokens,
        amask,
        pair,
        pmask,
        table,
        focus_gain[None, :],
        entry,
        exit_w,
        pair_gain[None, :],
        head_w.T,
        product_gain[None, :],
        prod_w.T,
        outer_w,
        tri_w,
        tri_gain[None, :],
        tri_out,
    )
    order = (3, 9, 10, 14, 4, 0, 1, 5, 6, 7, 13, 12, 2, 8, 11, 15, 16)
    owners = P_ // 2 * Q_
    per_dev = cz // owners
    unit = G * per_dev
    half = seqs * SUB
    seq_all = D_ * seqs
    f32, bf16 = jnp.float32, jnp.bfloat16
    vm = pltpu.VMEM
    dma = pltpu.SemaphoreType.DMA
    results = pl.pallas_call(
        functools.partial(staged_kernel, (P_, B_, K_), order),
        out_shape=(
            jax.ShapeDtypeStruct(feat.shape, bf16),
            jax.ShapeDtypeStruct(pair.shape, bf16),
        ),
        in_specs=[pl.BlockSpec(memory_space=pltpu.HBM)] * len(operands),
        out_specs=(pl.BlockSpec(memory_space=vm), pl.BlockSpec(memory_space=vm)),
        scratch_shapes=[
            vm((rows * cols, cz), bf16),
            vm((G * heads, LANES), f32),
            vm((D_, G * heads, LANES), f32),
            vm((2, owners, unit, LANES), bf16),
            vm((owners, unit, LANES), bf16),
            vm((D_, unit, LANES), bf16),
            vm((P_, half, LANES), bf16),
            vm((Q_, half, LANES), bf16),
            vm((D_, half, LANES), bf16),
            vm((D_, half, LANES), bf16),
            vm((owners, unit, LANES), bf16),
            vm((owners, unit, LANES), bf16),
            vm((fac * fac, LANES), f32),
            vm((res * per_dev, LANES), f32),
            vm((width // LANES, res, per * res), f32),
            vm((seqs * res, width), f32),
            vm((seqs, width // LANES, LANES, per * res), bf16),
            vm((seqs * res, width), bf16),
            vm((3 * width, width), bf16),
            vm((seqs, heads, width // heads + 16, res), bf16),
            vm((seqs * res, width), bf16),
            vm((width, seqs * res), f32),
            vm((seqs * res, LANES), f32),
            vm((seqs, width, res), f32),
            vm((width // LANES, seqs * res, LANES), f32),
            vm((cz, fac * fac), bf16),
            vm((G, LANES, LANES), f32),
            vm((nch * seq_all, fac * LANES), bf16),
            vm((G // 2, fac * fac, 2 * LANES), bf16),
            vm((-(-table.shape[0] // 16) * 16, width), f32),
            vm((nch * width, nch * fac), bf16),
            vm((G, LANES, cz), f32),
            dma,
            dma((P_,)),
            dma((P_,)),
            dma,
            dma((2,)),
            dma((2,)),
            dma,
            dma,
            dma,
            dma,
            dma,
            dma((P_,)),
            dma,
        ]
        + [vm(x.shape, x.dtype) for x in operands]
        + [dma((len(operands),))],
        compiler_params=pltpu.CompilerParams(collective_id=0, has_side_effects=True),
    )(*operands)
    return pl.pallas_call(
        settle_kernel,
        out_shape=tuple(jax.ShapeDtypeStruct(x.shape, x.dtype) for x in results),
        in_specs=[pl.BlockSpec(memory_space=pltpu.HBM)] * 2,
        out_specs=(pl.BlockSpec(memory_space=pltpu.HBM),) * 2,
        scratch_shapes=[vm(x.shape, x.dtype) for x in results] + [dma((4,))],
    )(*results)


def solution(mesh):
    in_specs = (
        P(("groups", "dap", "branch", "chan"), None, None),
        P(("groups", "dap", "branch", "chan"), None),
        P(("groups", "dap", "branch", "chan"), None),
        P(("groups", "dap"), ("branch", "chan"), None),
        P(("groups", "dap"), ("branch", "chan")),
        P(),
        P(),
        P(),
        P(),
        P(),
        P(),
        P(),
        P(),
        P(),
        P(),
        P(),
        P(),
    )
    out_specs = (
        P(("groups", "dap", "branch", "chan"), None, None),
        P(("groups", "dap"), ("branch", "chan"), None),
    )
    return jax.shard_map(fused, mesh=mesh, in_specs=in_specs, out_specs=out_specs, check_vma=False)
```

```python
import functools

import jax
import jax.numpy as jnp
from jax import lax
from jax.experimental import pallas as pl
from jax.experimental.pallas import tpu as pltpu
from jax.sharding import PartitionSpec as P


def layer_normalize(values, gain_vector, norm_axis):
    center = values - jnp.mean(values, axis=norm_axis, keepdims=True)
    spread = jnp.mean(center * center, axis=norm_axis, keepdims=True)
    return center * lax.rsqrt(spread + 1e-05) * gain_vector


def channel_products(left_part, right_part, dap_count, column_count, rows_block, column_block):
    row_ratio = dap_count // column_count
    channels_here = left_part.size // (dap_count * column_count * rows_block * column_block)
    left_five = left_part.reshape(dap_count, column_count, channels_here, rows_block, column_block)
    right_six = right_part.reshape(
        column_count, row_ratio, column_count, channels_here, rows_block, column_block
    )
    product = jnp.einsum(
        "pqrik,bhqrjk->pbrihj", left_five, right_six, preferred_element_type=jnp.float32
    )
    return product.astype(jnp.bfloat16)


def shards(
    homolog_features,
    alignment_tokens,
    alignment_mask,
    pair_activation_input,
    pair_residue_mask,
    letter_lookup_matrix,
    homolog_focus_scaling,
    focus_entry_matrix,
    focus_exit_matrix,
    pair_norm_gain,
    head_bias_weight,
    tensor_product_scaling,
    tensor_product_matrix,
    outer_output_weight,
    triangle_input_weight,
    triangle_norm_gain,
    triangle_output_weight,
):
    dap_count = lax.axis_size("dap")
    column_count = lax.axis_size("branch") * lax.axis_size("chan")
    device_count = dap_count * column_count
    rows_block, column_block, pair_width = pair_activation_input.shape
    sequence_total, residue_total, alignment_width = homolog_features.shape
    number_heads = head_bias_weight.shape[1]
    per_head_width = alignment_width // number_heads
    outer_factor_width = tensor_product_matrix.shape[1] // 2
    pair_normed = layer_normalize(
        pair_activation_input.astype(jnp.float32), pair_norm_gain, -1
    ).astype(jnp.bfloat16)
    bias_block = jnp.einsum(
        "ikc,ch->hik", pair_normed, head_bias_weight, preferred_element_type=jnp.float32
    )
    tri_linear = jnp.einsum(
        "ikc,ce->eik",
        pair_normed,
        triangle_input_weight[:, : 4 * pair_width],
        preferred_element_type=jnp.float32,
    )
    mask_pair = pair_residue_mask.astype(jnp.float32)
    tri_left = (
        jax.nn.sigmoid(tri_linear[pair_width : 2 * pair_width])
        * tri_linear[:pair_width]
        * mask_pair
    ).astype(jnp.bfloat16)
    tri_right = (
        jax.nn.sigmoid(tri_linear[3 * pair_width : 4 * pair_width])
        * tri_linear[2 * pair_width : 3 * pair_width]
        * mask_pair
    ).astype(jnp.bfloat16)
    out_gate = jnp.einsum(
        "ikc,ce->ike",
        pair_normed,
        triangle_input_weight[:, 4 * pair_width :],
        preferred_element_type=jnp.float32,
    )
    per_device = pair_width // device_count
    flat_shape = (device_count, 1, per_device, rows_block, column_block)
    products = channel_products(
        lax.all_to_all(
            tri_left.reshape(flat_shape),
            ("dap", "branch", "chan"),
            split_axis=0,
            concat_axis=1,
            tiled=True,
        ),
        lax.all_to_all(
            tri_right.reshape(flat_shape),
            ("dap", "branch", "chan"),
            split_axis=0,
            concat_axis=1,
            tiled=True,
        ),
        dap_count,
        column_count,
        rows_block,
        column_block,
    )
    channels_here = products.shape[2]
    sending = products.reshape(device_count, 1, channels_here, rows_block, column_block)
    returned = lax.all_to_all(
        sending, ("dap", "branch", "chan"), split_axis=0, concat_axis=1, tiled=True
    )
    tri_sum = returned.reshape(pair_width, rows_block, column_block)
    tri_normed = layer_normalize(
        tri_sum.astype(jnp.float32), triangle_norm_gain[:, None, None], 0
    ).astype(jnp.bfloat16)
    tri_update = jax.nn.sigmoid(out_gate) * jnp.einsum(
        "cik,ce->ike", tri_normed, triangle_output_weight, preferred_element_type=jnp.float32
    )
    token_class_count = letter_lookup_matrix.shape[0]
    token_indicator = (
        alignment_tokens[:, :, None] == jnp.arange(token_class_count, dtype=jnp.int32)
    ).astype(jnp.bfloat16)
    embedded_tokens = homolog_features.astype(jnp.float32) + jnp.einsum(
        "snv,vc->snc", token_indicator, letter_lookup_matrix, preferred_element_type=jnp.float32
    )
    alignment_normalized = layer_normalize(embedded_tokens, homolog_focus_scaling, -1).astype(
        jnp.bfloat16
    )
    projected_values = jnp.einsum(
        "rdz,zg->rdg", alignment_normalized, focus_entry_matrix, preferred_element_type=jnp.float32
    )
    query_rows = projected_values[:, :, :alignment_width].astype(jnp.bfloat16)
    every_key = projected_values[:, :, alignment_width : 2 * alignment_width].astype(jnp.bfloat16)
    every_value = projected_values[:, :, 2 * alignment_width : 3 * alignment_width].astype(
        jnp.bfloat16
    )
    gate_values = projected_values[:, :, 3 * alignment_width :]
    key_mask_bias = (alignment_mask.astype(jnp.float32) - 1.0) * 1000000000.0
    score_scale = per_head_width ** (-0.5)
    bias_partial = lax.all_gather(bias_block, ("branch", "chan"), axis=2, tiled=True)
    bias_full = lax.all_gather(bias_partial, "dap", axis=1, tiled=True)
    query_form = query_rows.reshape(sequence_total, residue_total, number_heads, per_head_width)
    key_form = every_key.reshape(sequence_total, residue_total, number_heads, per_head_width)
    value_form = every_value.reshape(sequence_total, residue_total, number_heads, per_head_width)
    mask_form = key_mask_bias.reshape(sequence_total, 1, 1, residue_total)

    def attend(seq_item):
        query_seq, key_seq, value_seq, mask_seq = seq_item
        scores = (
            jnp.einsum("ihd,jhd->hij", query_seq, key_seq, preferred_element_type=jnp.float32)
            * score_scale
            + bias_full
            + mask_seq
        )
        largest = jnp.max(scores, axis=2, keepdims=True)
        exponent = jnp.exp(scores - largest)
        attention_weights = (exponent / jnp.sum(exponent, axis=2, keepdims=True)).astype(
            jnp.bfloat16
        )
        return jnp.einsum(
            "bqo,obm->qbm", attention_weights, value_seq, preferred_element_type=jnp.float32
        )

    attended_rows = lax.map(attend, (query_form, key_form, value_form, mask_form)).reshape(
        sequence_total, residue_total, alignment_width
    )
    gated_output = (attended_rows * jax.nn.sigmoid(gate_values)).astype(jnp.bfloat16)
    alignment_output = (
        embedded_tokens
        + jnp.einsum(
            "rdz,zg->rdg", gated_output, focus_exit_matrix, preferred_element_type=jnp.float32
        )
    ).astype(jnp.bfloat16)
    outer_normalized = layer_normalize(
        alignment_output.astype(jnp.float32), tensor_product_scaling, -1
    ).astype(jnp.bfloat16)
    alignment_mask_rows = alignment_mask.astype(jnp.float32)[:, :, None]
    left_projection = (
        (
            jnp.einsum(
                "rdz,zg->rdg",
                outer_normalized,
                tensor_product_matrix[:, :outer_factor_width],
                preferred_element_type=jnp.float32,
            )
            * alignment_mask_rows
        )
        .astype(jnp.bfloat16)
        .reshape(sequence_total, residue_total * outer_factor_width)
    )
    right_projection = (
        (
            jnp.einsum(
                "rdz,zg->rdg",
                outer_normalized,
                tensor_product_matrix[:, outer_factor_width:],
                preferred_element_type=jnp.float32,
            )
            * alignment_mask_rows
        )
        .astype(jnp.bfloat16)
        .reshape(sequence_total, residue_total * outer_factor_width)
    )
    left_gathered, right_gathered = (
        lax.all_gather(left_projection, ("branch", "chan"), axis=0, tiled=True),
        lax.all_gather(right_projection, ("branch", "chan"), axis=0, tiled=True),
    )
    column_index = lax.axis_index("branch") * lax.axis_size("chan") + lax.axis_index("chan")
    right_block = lax.dynamic_slice_in_dim(
        right_gathered,
        column_index * (column_block * outer_factor_width),
        column_block * outer_factor_width,
        1,
    )
    left_block = lax.all_to_all(left_gathered, "dap", split_axis=1, concat_axis=0, tiled=True)
    right_full = lax.all_gather(right_block, "dap", axis=0, tiled=True)
    total_seqs = left_block.shape[0]
    outer = jnp.einsum(
        "sic,sjd->ijcd",
        left_block.reshape(total_seqs, rows_block, outer_factor_width),
        right_full.reshape(total_seqs, column_block, outer_factor_width),
        preferred_element_type=jnp.float32,
    ) * (1.0 / total_seqs)
    flat_outer = outer.astype(jnp.bfloat16).reshape(
        rows_block * column_block, outer_factor_width * outer_factor_width
    )
    outer_update = jnp.dot(
        flat_outer, outer_output_weight, preferred_element_type=jnp.float32
    ).reshape(rows_block, column_block, pair_width)
    pair_activation_output = (
        pair_activation_input.astype(jnp.float32) + tri_update + outer_update
    ).astype(jnp.bfloat16)
    return (alignment_output, pair_activation_output)


LANES = 128
SUB = 8
LOG2E = 1.4426950408889634


def dot_nn(left, right):
    return lax.dot_general(left, right, (((1,), (0,)), ((), ())), preferred_element_type=jnp.float32)


def dot_nt(left, right):
    return lax.dot_general(left, right, (((1,), (1,)), ((), ())), preferred_element_type=jnp.float32)


def chunk_swap(parts, width):
    parts = list(parts)
    lane = lax.broadcasted_iota(jnp.int32, parts[0].shape, parts[0].ndim - 1)
    axis = parts[0].ndim - 1
    step = len(parts) // 2
    while step >= 1:
        span = step * width
        low = (lane // span) % 2 == 0
        for a in range(len(parts)):
            if (a // step) % 2 == 0:
                lo, hi = parts[a], parts[a + step]
                parts[a] = jnp.where(low, lo, pltpu.roll(hi, span, axis))
                parts[a + step] = jnp.where(low, pltpu.roll(lo, LANES - span, axis), hi)
        step //= 2
    return parts


def norm_rows(values, gain):
    center = values - jnp.mean(values, axis=-1, keepdims=True)
    spread = jnp.mean(center * center, axis=-1, keepdims=True)
    return center * lax.rsqrt(spread + 1e-05) * gain


def half_sigmoid(values):
    return 0.5 * jnp.tanh(0.5 * values) + 0.5


def wide_stat(parts, ones, width):
    total = sum(dot_nn(x, ones) for x in parts) * (1.0 / width)
    return jnp.concatenate([total] * (width // LANES), axis=1)


def norm_mxu(values, parts, gain, ones):
    width = values.shape[1]
    center = values - wide_stat(parts, ones, width)
    spread = wide_stat([(center * center).astype(jnp.bfloat16)], ones, width)
    return center * lax.rsqrt(spread + 1e-05) * gain


def staged_kernel(sizes, order, *refs):
    count = len(order)
    sources, rest = refs[:count], refs[count : len(refs) - count - 1]
    held, sems = refs[len(refs) - count - 1 : -1], refs[-1]
    fetches = [pltpu.make_async_copy(sources[i], held[i], sems.at[i]) for i in range(count)]

    def begin():
        for i in order:
            fetches[i].start()

    def ready(*which):
        for i in which:
            fetches[i].wait()

    block_kernel(sizes, begin, ready, *held, *rest)


def block_kernel(
    sizes,
    begin,
    ready,
    feat,
    tokens,
    amask,
    pair,
    pmask,
    table,
    focus_gain,
    entry,
    exit_w,
    pair_gain,
    head_t,
    product_gain,
    prod_t,
    outer_w,
    tri_w,
    tri_gain,
    tri_out,
    align_out,
    pair_out,
    pn,
    bsend,
    brecv,
    tsend,
    trecv_l,
    trecv_r,
    lsend,
    rsend,
    lrecv,
    rrecv,
    zsend,
    zrecv,
    stage_a,
    stage_b,
    stage_z,
    bias_full,
    emb,
    qd,
    keys,
    entry_t,
    vt,
    rows_n,
    att_t,
    mask_c,
    gates,
    normed,
    w2t,
    upd,
    rblk,
    obuf,
    table_f,
    left_w,
    gate_f,
    b_send,
    b_z,
    b_x,
    b_c,
    t_send,
    t_recv,
    o_send,
    o_recv,
    o_z,
    o_f,
    z_send,
    z_recv,
    l_send,
    l_z,
    l_recv,
    row_in,
):
    P_, B_, K_ = sizes
    Q_ = B_ * K_
    D_ = P_ * Q_
    rows, cols, cz = pair.shape
    seqs, res, width = feat.shape
    heads = head_t.shape[0]
    hw = width // heads
    per = LANES // hw
    groups = width // LANES
    fac = prod_t.shape[0] // 2
    nch = LANES // cols
    G = rows // nch
    mp = lax.axis_index("dap")
    mb = lax.axis_index("branch")
    mk = lax.axis_index("chan")
    mq = mb * K_ + mk
    me = mp * Q_ + mq

    def peer(off):
        dp, db, dk = off // Q_, (off // K_) % B_, off % K_
        p, b, k = mp ^ dp, mb ^ db, mk ^ dk
        return p, b * K_ + k, {"dap": p, "branch": b, "chan": k}

    def remote(src, dst, ss, rs, dev):
        return pltpu.make_async_remote_copy(
            src_ref=src,
            dst_ref=dst,
            send_sem=ss,
            recv_sem=rs,
            device_id=dev,
            device_id_type=pl.DeviceIdType.MESH,
        )

    here_dev = peer(1)[2]

    def sent(ref, sem):
        remote(ref, ref, sem, sem, here_dev).wait_send()

    def arrived(ref, sem):
        remote(ref, ref, sem, sem, here_dev).wait_recv()

    def exchange(send, recv, ss, rs, offs):
        for off in offs:
            p, q, dev = peer(off)
            remote(send(p, q), recv.at[me], ss, rs, dev).start()

    z_offs = [op * Q_ for op in range(1, P_)]
    q_offs = list(range(1, Q_))
    all_offs = sorted(range(1, D_), key=lambda off: (-(off // Q_), off % Q_))

    half_p = P_ // 2
    begin()
    barrier = pltpu.get_barrier_semaphore()
    for off in z_offs + q_offs:
        pl.semaphore_signal(
            barrier, inc=1, device_id=peer(off)[2], device_id_type=pl.DeviceIdType.MESH
        )

    ready(3, 9)
    pair_h = pair[...].reshape(rows * cols, cz)
    ones_z = jnp.ones((cz, LANES), jnp.bfloat16)
    pn[...] = norm_mxu(pair_h.astype(jnp.float32), [pair_h], pair_gain[...], ones_z).astype(
        jnp.bfloat16
    )

    def pair_rows(g):
        return jnp.concatenate(
            [pn[(a * G + g) * cols : (a * G + g + 1) * cols, :] for a in range(nch)], axis=0
        )

    ready(10)
    for g in range(G):
        stage_b[g * heads : (g + 1) * heads, :] = dot_nt(head_t[...], pair_rows(g)) * LOG2E
    for b in range(groups):
        pieces = []
        for h in range(per):
            by_head = stage_b[pl.ds(b * per + h, G, stride=heads), :]
            for a in range(nch):
                pieces.append(pltpu.roll(by_head, LANES - a * cols, 1) if a else by_head)
        bsend[b * cols : (b + 1) * cols, :] = jnp.concatenate(pieces, axis=0).T[:cols]
    brecv[me] = bsend[...]
    pl.semaphore_wait(barrier, P_ + Q_ - 2)
    for off in z_offs:
        pl.semaphore_signal(
            row_in, inc=1, device_id=peer(off)[2], device_id_type=pl.DeviceIdType.MESH
        )
    for op in range(1, P_):
        p, q, dev = peer(op * Q_)
        remote(bsend, brecv.at[me], b_send, b_z.at[op], dev).start()
    xoff = K_

    def pass_on(src, slot, sem, off):
        remote(src, brecv.at[slot], b_send, sem, peer(off)[2]).start()

    pass_on(bsend, me, b_x.at[0], xoff)
    pass_on(bsend, me, b_c, 1)
    owners = half_p * Q_
    parts_n = 2
    per_dev = cz // (owners * parts_n)
    unit = G * per_dev
    mine = (mp % half_p) * Q_ + mq
    ready(4, 14)
    mrows = jnp.concatenate(
        [pmask[a * G : (a + 1) * G, :].astype(jnp.float32) for a in range(nch)], axis=1
    )
    trecv = (trecv_l, trecv_r)

    def tri_factor(side):
        at = 2 * side * cz
        tri_t = tri_w[:, at : at + 2 * cz].astype(jnp.float32).T.astype(jnp.bfloat16)
        for t in range(G // 2):
            block = jnp.concatenate([pair_rows(2 * t), pair_rows(2 * t + 1)], axis=0)
            lin = dot_nt(tri_t, block)
            mrow = jnp.concatenate([mrows[2 * t : 2 * t + 1], mrows[2 * t + 1 : 2 * t + 2]], axis=1)
            val = half_sigmoid(lin[cz:]) * (lin[:cz] * mrow)
            for n in range(owners):
                for h in range(parts_n):
                    at_c = (n * parts_n + h) * per_dev
                    piece = val[at_c : at_c + per_dev]
                    two = jnp.concatenate([piece[:, :LANES], piece[:, LANES:]], axis=0)
                    tsend[side, h, n, 2 * t * per_dev : 2 * (t + 1) * per_dev, :] = two.astype(
                        jnp.bfloat16
                    )
        for h in range(parts_n):
            if side == 0:
                trecv_l[h, mine] = tsend[side, h, mine]
            else:
                trecv_r[h, me] = tsend[side, h, mine]

    def tri_send(side, h, offs):
        for off in offs:
            p, q, dev = peer(off)
            slot = mine if side == 0 else me
            remote(
                tsend.at[side, h, (p % half_p) * Q_ + q],
                trecv[side].at[h, slot],
                t_send.at[side],
                t_recv.at[side, h],
                dev,
            ).start()

    in_half = [off for off in range(1, D_) if off // Q_ < half_p]
    far = [off for off in range(1, D_) if off // Q_ >= half_p]
    own_row = [off for off in in_half if off < Q_]
    next_row = [off for off in in_half if off >= Q_]
    same_x = lambda offs: [off for off in offs if (off // K_) % B_ == 0]
    other_x = lambda offs: [off for off in offs if (off // K_) % B_ == 1]
    tri_factor(1)
    pl.semaphore_wait(row_in, P_ - 1)
    for h in range(parts_n):
        tri_send(1, h, same_x(far))
    tri_factor(0)
    for h in range(parts_n):
        tri_send(1, h, in_half)
        tri_send(0, h, in_half)

    ready(0, 1, 2, 5, 6, 7, 8, 11, 12, 13, 15, 16)
    table_f[...] = jnp.zeros_like(table_f)
    table_f[: table.shape[0], :] = table[...].astype(jnp.float32)
    table_all = table_f[...].astype(jnp.bfloat16)
    kinds_n = table_f.shape[0]
    ones_m = jnp.ones((width, LANES), jnp.bfloat16)
    scale = hw ** (-0.5) * LOG2E
    for n, at in enumerate((0, 2 * width, 3 * width)):
        part = entry[:, at : at + width].astype(jnp.float32).T
        entry_t[n * width : (n + 1) * width, :] = part.astype(jnp.bfloat16)
    qd[...] = jnp.zeros_like(qd)
    for s in range(seqs):
        for h in range(heads):
            vt[s, h, hw:, :] = jnp.ones((vt.shape[2] - hw, res), jnp.bfloat16)
    kinds = lax.broadcasted_iota(jnp.int32, (kinds_n, res), 0)
    hot = jnp.concatenate(
        [jnp.where(kinds == tokens[s : s + 1, :], 1.0, 0.0) for s in range(seqs)], axis=1
    ).astype(jnp.float32)
    here = feat[...].astype(jnp.float32).reshape(seqs * res, width)
    here = here + dot_nn(hot.T.astype(jnp.bfloat16), table_all)
    emb[...] = here
    high = here.astype(jnp.bfloat16)
    low = (here - high.astype(jnp.float32)).astype(jnp.bfloat16)
    rows_n[...] = norm_mxu(here, [high, low], focus_gain[...], ones_m).astype(jnp.bfloat16)
    keys[...] = dot_nn(rows_n[...], entry[:, width : 2 * width]).astype(jnp.bfloat16)
    for u in range(seqs // 2):
        two = rows_n[2 * u * res : 2 * (u + 1) * res, :]
        for n in range(3):
            turned = dot_nt(entry_t[n * width : (n + 1) * width, :], two)
            for v in range(2):
                s = 2 * u + v
                here = turned[:, v * res : (v + 1) * res]
                if n == 2:
                    gates[s] = half_sigmoid(here)
                    continue
                for h in range(heads):
                    b, e = h // per, h % per
                    part = here[h * hw : (h + 1) * hw]
                    if n == 0:
                        qd[s, b, e * hw : (e + 1) * hw, e * res : (e + 1) * res] = (
                            part * scale
                        ).astype(jnp.bfloat16)
                    else:
                        vt[s, h, :hw, :] = part.astype(jnp.bfloat16)

    for op in range(1, P_):
        arrived(bsend, b_z.at[op])
        slot = (mp ^ op) * Q_ + mq
        pass_on(brecv.at[slot], slot, b_x.at[op], xoff)
        pass_on(brecv.at[slot], slot, b_c, 1)
    for h in range(parts_n):
        tri_send(1, h, other_x(far))

    four = jnp.concatenate([prod_t[:fac, :].astype(jnp.float32)] * nch, axis=0).T
    lane_fac = lax.broadcasted_iota(jnp.int32, four.shape, 1) // fac
    for a in range(nch):
        left_w[a * width : (a + 1) * width, :] = jnp.where(lane_fac == a, four, 0.0).astype(
            jnp.bfloat16
        )
    for g in range(G):
        gate_f[g] = half_sigmoid(dot_nn(pair_rows(g), tri_w[:, 4 * cz :]))
    stage_a[...] = outer_w[...].astype(jnp.float32)
    for g in range(SUB):
        piece = jnp.concatenate(
            [stage_a[pl.ds(a * SUB + g, fac, stride=fac), :] for a in range(fac // SUB)], axis=0
        )
        w2t[:, g * LANES : (g + 1) * LANES] = piece.T.astype(jnp.bfloat16)

    for op in range(P_):
        arrived(bsend, b_x.at[op])
        slot = (mp ^ op) * Q_ + (mb ^ 1) * K_ + mk
        pass_on(brecv.at[slot], slot, b_c, 1)
    arrived(brecv.at[: 2 * P_], b_c)
    for q in range(Q_):
        for b in range(groups):
            got = chunk_swap(
                [brecv[p * Q_ + q, b * cols : (b + 1) * cols, :] for p in range(P_)], cols
            )
            for h in range(per):
                bias_full[b, q * cols : (q + 1) * cols, h * res : (h + 1) * res] = got[h]

    for s in range(seqs):
        mcol = jnp.broadcast_to(amask[s : s + 1, :].astype(jnp.float32), (res, res)).T
        mask_add = (mcol - 1.0) * (1000000000.0 * LOG2E)
        for h in range(heads):
            b, e = h // per, h % per
            sl = slice(e * res, (e + 1) * res)
            sc = dot_nn(
                keys[s * res : (s + 1) * res, b * LANES : (b + 1) * LANES], qd[s, b, :, sl]
            )
            sc = (sc + bias_full[b, :, sl]) + mask_add
            ex = jnp.exp2(sc - jnp.max(sc, axis=0, keepdims=True)).astype(jnp.bfloat16)
            av = dot_nn(vt[s, h], ex)
            att_t[h * hw : (h + 1) * hw, s * res : (s + 1) * res] = (
                av[:hw] * (1.0 / av[hw : hw + 1]) * gates[s, h * hw : (h + 1) * hw, :]
            )
        mask_c[s * res : (s + 1) * res, :] = mcol
    attended = att_t[...].T.astype(jnp.bfloat16)
    out = (emb[...] + dot_nn(attended, exit_w[...])).astype(jnp.bfloat16)
    align_out[...] = out.reshape(seqs, res, width)
    on = norm_mxu(out.astype(jnp.float32), [out], product_gain[...], ones_m)
    on = on.astype(jnp.bfloat16).astype(jnp.float32)
    for b in range(groups):
        normed[b] = on[:, b * LANES : (b + 1) * LANES] * mask_c[...]

    each = seqs * res // nch
    wide = [
        normed[b, pl.ds(a, each, stride=nch), :].astype(jnp.bfloat16)
        for a in range(nch)
        for b in range(groups)
    ]
    left = dot_nn(jnp.concatenate(wide, axis=1), left_w[...])
    rows_all = jnp.concatenate([normed[b] for b in range(groups)], axis=1).astype(jnp.bfloat16)
    right = dot_nt(prod_t[fac:, :], rows_all)
    lefts = [
        jnp.concatenate(
            [left[(s * P_ + p) * G : (s * P_ + p + 1) * G] for s in range(seqs)], axis=0
        ).astype(jnp.bfloat16)
        for p in range(P_)
    ]
    by_seq = []
    for s in range(seqs):
        by_seq.append(
            chunk_swap(
                [right[a * SUB : (a + 1) * SUB, s * res : (s + 1) * res] for a in range(nch)], cols
            )
        )
    half = seqs * SUB
    for p in range(P_):
        lsend[p] = lefts[p]
    for q in range(Q_):
        rsend[q] = jnp.concatenate([by_seq[s][q] for s in range(seqs)], axis=0).astype(jnp.bfloat16)
    lrecv[me] = lsend[mp]
    rrecv[me] = rsend[mq]
    for op in range(1, P_):
        p, q, dev = peer(op * Q_)
        remote(lsend.at[p], lrecv.at[me], l_send, l_z.at[op], dev).start()
    exchange(lambda p, q: lsend.at[mp], lrecv, l_send, l_recv, q_offs)
    cross = [off for off in all_offs if off // Q_ == half_p]
    exchange(lambda p, q: rsend.at[q], rrecv, o_send, o_z, cross)
    exchange(lambda p, q: rsend.at[q], rrecv, o_send, o_recv, [off for off in all_offs if off // Q_ < half_p])

    def tri_sums(h):
        for side, stage in enumerate((stage_a, stage_b)):
            arrived(trecv[side].at[h, : (owners if side == 0 else D_) - 1], t_recv.at[side, h])
            for p in range(half_p if side == 0 else P_):
                got = chunk_swap(
                    [trecv[side][h, p * Q_ + q].astype(jnp.float32) for q in range(Q_)],
                    cols,
                )
                for a in range(nch):
                    stage[(p * nch + a) * unit : (p * nch + a + 1) * unit, :] = got[a]
        for c in range(per_dev):
            lc = stage_a[pl.ds(c, half_p * rows, stride=per_dev), :].astype(jnp.bfloat16)
            rc = stage_b[pl.ds(c, res, stride=per_dev), :].astype(jnp.bfloat16)
            z = dot_nt(lc, rc)
            for p in range(half_p):
                got = chunk_swap(
                    [z[(p * nch + a) * G : (p * nch + a + 1) * G] for a in range(nch)], cols
                )
                for q in range(Q_):
                    stage_z[pl.ds((p * Q_ + q) * unit + c, G, stride=per_dev), :] = got[q]
        for n in range(owners):
            zsend[h, n] = stage_z[n * unit : (n + 1) * unit, :].astype(jnp.bfloat16)
        zrecv[h, mine] = zsend[h, mine]
        for off in sorted(in_half, reverse=True):
            p, q, dev = peer(off)
            remote(
                zsend.at[h, (p % half_p) * Q_ + q], zrecv.at[h, mine], z_send, z_recv.at[h], dev
            ).start()

    for h in range(parts_n):
        tri_sums(h)
        if h == 0:
            for op in range(1, P_):
                arrived(lsend.at[0], l_z.at[op])
                slot = (mp ^ op) * Q_ + mq
                for off in q_offs:
                    remote(
                        lrecv.at[slot], lrecv.at[slot], l_send, l_recv, peer(off)[2]
                    ).start()
            arrived(rrecv.at[:Q_], o_z)
            theirs = pl.ds((mp ^ half_p) * Q_, Q_)
            remote(rrecv.at[theirs], rrecv.at[theirs], o_send, o_f, peer(Q_)[2]).start()

    arrived(lrecv.at[: P_ * (Q_ - 1)], l_recv)
    arrived(rrecv.at[: half_p * Q_ - 1], o_recv)
    arrived(rrecv.at[:Q_], o_f)
    total = D_ * half
    for n in range(D_):
        stage_a[n * half : (n + 1) * half, :] = lrecv[n].astype(jnp.float32)
        stage_b[n * half : (n + 1) * half, :] = rrecv[n].astype(jnp.float32)
    seq_all = D_ * seqs
    gh = G // nch
    lhs = jnp.concatenate(
        [
            jnp.concatenate(
                [stage_a[pl.ds(a * gh + h, seq_all, stride=SUB), :] for a in range(nch)], axis=0
            ).T
            for h in range(gh)
        ],
        axis=0,
    ).astype(jnp.bfloat16)
    lane_col = lax.broadcasted_iota(jnp.int32, (seq_all, LANES), 1) // cols
    keep = [jnp.where(lane_col == a, 1.0, 0.0).astype(jnp.bfloat16) for a in range(nch)]
    for k in range(SUB):
        here = stage_b[pl.ds(k, seq_all, stride=SUB), :]
        turned = [here] + [pltpu.roll(here, r * cols, 1) for r in range(1, nch)]
        turned = [x.astype(jnp.bfloat16) for x in turned]
        for d in range(nch):
            at = (k * nch + d) * LANES
            for a in range(nch):
                rblk[a * seq_all : (a + 1) * seq_all, at : at + LANES] = (
                    turned[(a - d) % nch] * keep[a]
                )
        for t in range(k * nch // 2, (k + 1) * nch // 2):
            prod = dot_nn(lhs, rblk[:, 2 * t * LANES : 2 * (t + 1) * LANES]).astype(jnp.bfloat16)
            for g in range(G):
                for e in range(2):
                    obuf[g // 2, (2 * t + e) * fac : (2 * t + e + 1) * fac, (g % 2) * LANES : (g % 2 + 1) * LANES] = prod[
                        g * fac : (g + 1) * fac, e * LANES : (e + 1) * LANES
                    ]
    for t in range(G // 2):
        both = dot_nn(w2t[...], obuf[t]) * (1.0 / seq_all)
        for e in range(2):
            g = 2 * t + e
            up = both[:, e * LANES : (e + 1) * LANES].T
            for a in range(nch):
                sl = slice(a * cols, (a + 1) * cols)
                upd[g, sl, :] = pair[a * G + g].astype(jnp.float32) + up[sl]

    sent(brecv.at[: D_ - 1], b_send)
    sent(trecv_l.at[:, : owners - 1], t_send.at[0])
    sent(trecv_r.at[:, : D_ - 1], t_send.at[1])
    sent(lrecv.at[: D_ - 1], l_send)
    sent(rrecv.at[: D_ - 1], o_send)
    for h in range(parts_n):
        arrived(zrecv.at[h, : owners - 1], z_recv.at[h])
    for n in range(owners):
        for h in range(parts_n):
            at_c = (n * parts_n + h) * unit
            stage_a[at_c : at_c + unit, :] = zrecv[h, n].astype(jnp.float32)
    for g in range(G):
        sums_g = jnp.concatenate(
            [
                stage_a[n * unit + g * per_dev : n * unit + (g + 1) * per_dev, :]
                for n in range(owners * parts_n)
            ],
            axis=0,
        ).T
        tn = norm_rows(sums_g, tri_gain[...]).astype(jnp.bfloat16)
        both = upd[g] + gate_f[g] * dot_nn(tn, tri_out[...])
        for a in range(nch):
            i = a * G + g
            sl = slice(a * cols, (a + 1) * cols)
            pair_out[i] = both[sl].astype(jnp.bfloat16)
    sent(zrecv.at[:, : owners - 1], z_send)


def settle_kernel(one, two, one_out, two_out, one_held, two_held, sems):
    come = [
        pltpu.make_async_copy(one, one_held, sems.at[0]),
        pltpu.make_async_copy(two, two_held, sems.at[1]),
    ]
    go = [
        pltpu.make_async_copy(one_held, one_out, sems.at[2]),
        pltpu.make_async_copy(two_held, two_out, sems.at[3]),
    ]
    for c in come:
        c.start()
    for c, d in zip(come, go):
        c.wait()
        d.start()
    for d in go:
        d.wait()


def kernel_fits(P_, B_, K_, args):
    Q_ = B_ * K_
    feat, pair, head_w, prod_w = args[0], args[3], args[10], args[12]
    rows, cols, cz = pair.shape
    seqs, res, width = feat.shape
    heads = head_w.shape[1]
    fac = prod_w.shape[1] // 2
    nch = LANES // cols
    return (
        res == LANES
        and cz == LANES
        and rows == cols
        and fac == cols
        and nch == P_
        and nch == Q_
        and rows == nch * SUB
        and cz == P_ * Q_ * SUB
        and heads == SUB
        and width % LANES == 0
        and width // heads == cols
        and D_rows(P_, Q_, seqs) <= fac * fac
        and P_ == 4
        and B_ == 2
        and K_ == 2
    )


def D_rows(P_, Q_, seqs):
    return P_ * Q_ * seqs * SUB


def fused(*args):
    P_ = lax.axis_size("dap")
    B_ = lax.axis_size("branch")
    K_ = lax.axis_size("chan")
    Q_ = B_ * K_
    D_ = P_ * Q_
    if not kernel_fits(P_, B_, K_, args):
        return shards(*args)
    (feat, tokens, amask, pair, pmask, table, focus_gain, entry, exit_w, pair_gain, head_w) = args[:11]
    (product_gain, prod_w, outer_w, tri_w, tri_gain, tri_out) = args[11:]
    rows, cols, cz = pair.shape
    seqs, res, width = feat.shape
    heads = head_w.shape[1]
    fac = prod_w.shape[1] // 2
    nch = LANES // cols
    G = rows // nch
    per = LANES // (width // heads)
    operands = (
        feat,
        tokens,
        amask,
        pair,
        pmask,
        table,
        focus_gain[None, :],
        entry,
        exit_w,
        pair_gain[None, :],
        head_w.T,
        product_gain[None, :],
        prod_w.T,
        outer_w,
        tri_w,
        tri_gain[None, :],
        tri_out,
    )
    order = (3, 9, 10, 14, 4, 0, 1, 5, 6, 7, 13, 12, 2, 8, 11, 15, 16)
    owners = P_ // 2 * Q_
    parts_n = 2
    per_dev = cz // (owners * parts_n)
    unit = G * per_dev
    half = seqs * SUB
    seq_all = D_ * seqs
    f32, bf16 = jnp.float32, jnp.bfloat16
    vm = pltpu.VMEM
    dma = pltpu.SemaphoreType.DMA
    results = pl.pallas_call(
        functools.partial(staged_kernel, (P_, B_, K_), order),
        out_shape=(
            jax.ShapeDtypeStruct(feat.shape, bf16),
            jax.ShapeDtypeStruct(pair.shape, bf16),
        ),
        in_specs=[pl.BlockSpec(memory_space=pltpu.HBM)] * len(operands),
        out_specs=(pl.BlockSpec(memory_space=vm), pl.BlockSpec(memory_space=vm)),
        scratch_shapes=[
            vm((rows * cols, cz), bf16),
            vm((G * heads, LANES), f32),
            vm((D_, G * heads, LANES), f32),
            vm((2, parts_n, owners, unit, LANES), bf16),
            vm((parts_n, owners, unit, LANES), bf16),
            vm((parts_n, D_, unit, LANES), bf16),
            vm((P_, half, LANES), bf16),
            vm((Q_, half, LANES), bf16),
            vm((D_, half, LANES), bf16),
            vm((D_, half, LANES), bf16),
            vm((parts_n, owners, unit, LANES), bf16),
            vm((parts_n, owners, unit, LANES), bf16),
            vm((fac * fac, LANES), f32),
            vm((fac * fac, LANES), f32),
            vm((owners * unit, LANES), f32),
            vm((width // LANES, res, per * res), f32),
            vm((seqs * res, width), f32),
            vm((seqs, width // LANES, LANES, per * res), bf16),
            vm((seqs * res, width), bf16),
            vm((3 * width, width), bf16),
            vm((seqs, heads, width // heads + 16, res), bf16),
            vm((seqs * res, width), bf16),
            vm((width, seqs * res), f32),
            vm((seqs * res, LANES), f32),
            vm((seqs, width, res), f32),
            vm((width // LANES, seqs * res, LANES), f32),
            vm((cz, fac * fac), bf16),
            vm((G, LANES, LANES), f32),
            vm((nch * seq_all, fac * LANES), bf16),
            vm((G // 2, fac * fac, 2 * LANES), bf16),
            vm((-(-table.shape[0] // 16) * 16, width), f32),
            vm((nch * width, nch * fac), bf16),
            vm((G, LANES, cz), f32),
            dma,
            dma((P_,)),
            dma((P_,)),
            dma,
            dma((2,)),
            dma((2, parts_n)),
            dma,
            dma,
            dma,
            dma,
            dma,
            dma((parts_n,)),
            dma,
            dma((P_,)),
            dma,
            pltpu.SemaphoreType.REGULAR,
        ]
        + [vm(x.shape, x.dtype) for x in operands]
        + [dma((len(operands),))],
        compiler_params=pltpu.CompilerParams(collective_id=0, has_side_effects=True),
    )(*operands)
    return pl.pallas_call(
        settle_kernel,
        out_shape=tuple(jax.ShapeDtypeStruct(x.shape, x.dtype) for x in results),
        in_specs=[pl.BlockSpec(memory_space=pltpu.HBM)] * 2,
        out_specs=(pl.BlockSpec(memory_space=pltpu.HBM),) * 2,
        scratch_shapes=[vm(x.shape, x.dtype) for x in results] + [dma((4,))],
    )(*results)


def solution(mesh):
    in_specs = (
        P(("groups", "dap", "branch", "chan"), None, None),
        P(("groups", "dap", "branch", "chan"), None),
        P(("groups", "dap", "branch", "chan"), None),
        P(("groups", "dap"), ("branch", "chan"), None),
        P(("groups", "dap"), ("branch", "chan")),
        P(),
        P(),
        P(),
        P(),
        P(),
        P(),
        P(),
        P(),
        P(),
        P(),
        P(),
        P(),
    )
    out_specs = (
        P(("groups", "dap", "branch", "chan"), None, None),
        P(("groups", "dap"), ("branch", "chan"), None),
    )
    return jax.shard_map(fused, mesh=mesh, in_specs=in_specs, out_specs=out_specs, check_vma=False)
```

```python
import functools

import jax
import jax.numpy as jnp
from jax import lax
from jax.experimental import pallas as pl
from jax.experimental.pallas import tpu as pltpu
from jax.sharding import PartitionSpec as P


def layer_normalize(values, gain_vector, norm_axis):
    center = values - jnp.mean(values, axis=norm_axis, keepdims=True)
    spread = jnp.mean(center * center, axis=norm_axis, keepdims=True)
    return center * lax.rsqrt(spread + 1e-05) * gain_vector


def channel_products(left_part, right_part, dap_count, column_count, rows_block, column_block):
    row_ratio = dap_count // column_count
    channels_here = left_part.size // (dap_count * column_count * rows_block * column_block)
    left_five = left_part.reshape(dap_count, column_count, channels_here, rows_block, column_block)
    right_six = right_part.reshape(
        column_count, row_ratio, column_count, channels_here, rows_block, column_block
    )
    product = jnp.einsum(
        "pqrik,bhqrjk->pbrihj", left_five, right_six, preferred_element_type=jnp.float32
    )
    return product.astype(jnp.bfloat16)


def shards(
    homolog_features,
    alignment_tokens,
    alignment_mask,
    pair_activation_input,
    pair_residue_mask,
    letter_lookup_matrix,
    homolog_focus_scaling,
    focus_entry_matrix,
    focus_exit_matrix,
    pair_norm_gain,
    head_bias_weight,
    tensor_product_scaling,
    tensor_product_matrix,
    outer_output_weight,
    triangle_input_weight,
    triangle_norm_gain,
    triangle_output_weight,
):
    dap_count = lax.axis_size("dap")
    column_count = lax.axis_size("branch") * lax.axis_size("chan")
    device_count = dap_count * column_count
    rows_block, column_block, pair_width = pair_activation_input.shape
    sequence_total, residue_total, alignment_width = homolog_features.shape
    number_heads = head_bias_weight.shape[1]
    per_head_width = alignment_width // number_heads
    outer_factor_width = tensor_product_matrix.shape[1] // 2
    pair_normed = layer_normalize(
        pair_activation_input.astype(jnp.float32), pair_norm_gain, -1
    ).astype(jnp.bfloat16)
    bias_block = jnp.einsum(
        "ikc,ch->hik", pair_normed, head_bias_weight, preferred_element_type=jnp.float32
    )
    tri_linear = jnp.einsum(
        "ikc,ce->eik",
        pair_normed,
        triangle_input_weight[:, : 4 * pair_width],
        preferred_element_type=jnp.float32,
    )
    mask_pair = pair_residue_mask.astype(jnp.float32)
    tri_left = (
        jax.nn.sigmoid(tri_linear[pair_width : 2 * pair_width])
        * tri_linear[:pair_width]
        * mask_pair
    ).astype(jnp.bfloat16)
    tri_right = (
        jax.nn.sigmoid(tri_linear[3 * pair_width : 4 * pair_width])
        * tri_linear[2 * pair_width : 3 * pair_width]
        * mask_pair
    ).astype(jnp.bfloat16)
    out_gate = jnp.einsum(
        "ikc,ce->ike",
        pair_normed,
        triangle_input_weight[:, 4 * pair_width :],
        preferred_element_type=jnp.float32,
    )
    per_device = pair_width // device_count
    flat_shape = (device_count, 1, per_device, rows_block, column_block)
    products = channel_products(
        lax.all_to_all(
            tri_left.reshape(flat_shape),
            ("dap", "branch", "chan"),
            split_axis=0,
            concat_axis=1,
            tiled=True,
        ),
        lax.all_to_all(
            tri_right.reshape(flat_shape),
            ("dap", "branch", "chan"),
            split_axis=0,
            concat_axis=1,
            tiled=True,
        ),
        dap_count,
        column_count,
        rows_block,
        column_block,
    )
    channels_here = products.shape[2]
    sending = products.reshape(device_count, 1, channels_here, rows_block, column_block)
    returned = lax.all_to_all(
        sending, ("dap", "branch", "chan"), split_axis=0, concat_axis=1, tiled=True
    )
    tri_sum = returned.reshape(pair_width, rows_block, column_block)
    tri_normed = layer_normalize(
        tri_sum.astype(jnp.float32), triangle_norm_gain[:, None, None], 0
    ).astype(jnp.bfloat16)
    tri_update = jax.nn.sigmoid(out_gate) * jnp.einsum(
        "cik,ce->ike", tri_normed, triangle_output_weight, preferred_element_type=jnp.float32
    )
    token_class_count = letter_lookup_matrix.shape[0]
    token_indicator = (
        alignment_tokens[:, :, None] == jnp.arange(token_class_count, dtype=jnp.int32)
    ).astype(jnp.bfloat16)
    embedded_tokens = homolog_features.astype(jnp.float32) + jnp.einsum(
        "snv,vc->snc", token_indicator, letter_lookup_matrix, preferred_element_type=jnp.float32
    )
    alignment_normalized = layer_normalize(embedded_tokens, homolog_focus_scaling, -1).astype(
        jnp.bfloat16
    )
    projected_values = jnp.einsum(
        "rdz,zg->rdg", alignment_normalized, focus_entry_matrix, preferred_element_type=jnp.float32
    )
    query_rows = projected_values[:, :, :alignment_width].astype(jnp.bfloat16)
    every_key = projected_values[:, :, alignment_width : 2 * alignment_width].astype(jnp.bfloat16)
    every_value = projected_values[:, :, 2 * alignment_width : 3 * alignment_width].astype(
        jnp.bfloat16
    )
    gate_values = projected_values[:, :, 3 * alignment_width :]
    key_mask_bias = (alignment_mask.astype(jnp.float32) - 1.0) * 1000000000.0
    score_scale = per_head_width ** (-0.5)
    bias_partial = lax.all_gather(bias_block, ("branch", "chan"), axis=2, tiled=True)
    bias_full = lax.all_gather(bias_partial, "dap", axis=1, tiled=True)
    query_form = query_rows.reshape(sequence_total, residue_total, number_heads, per_head_width)
    key_form = every_key.reshape(sequence_total, residue_total, number_heads, per_head_width)
    value_form = every_value.reshape(sequence_total, residue_total, number_heads, per_head_width)
    mask_form = key_mask_bias.reshape(sequence_total, 1, 1, residue_total)

    def attend(seq_item):
        query_seq, key_seq, value_seq, mask_seq = seq_item
        scores = (
            jnp.einsum("ihd,jhd->hij", query_seq, key_seq, preferred_element_type=jnp.float32)
            * score_scale
            + bias_full
            + mask_seq
        )
        largest = jnp.max(scores, axis=2, keepdims=True)
        exponent = jnp.exp(scores - largest)
        attention_weights = (exponent / jnp.sum(exponent, axis=2, keepdims=True)).astype(
            jnp.bfloat16
        )
        return jnp.einsum(
            "bqo,obm->qbm", attention_weights, value_seq, preferred_element_type=jnp.float32
        )

    attended_rows = lax.map(attend, (query_form, key_form, value_form, mask_form)).reshape(
        sequence_total, residue_total, alignment_width
    )
    gated_output = (attended_rows * jax.nn.sigmoid(gate_values)).astype(jnp.bfloat16)
    alignment_output = (
        embedded_tokens
        + jnp.einsum(
            "rdz,zg->rdg", gated_output, focus_exit_matrix, preferred_element_type=jnp.float32
        )
    ).astype(jnp.bfloat16)
    outer_normalized = layer_normalize(
        alignment_output.astype(jnp.float32), tensor_product_scaling, -1
    ).astype(jnp.bfloat16)
    alignment_mask_rows = alignment_mask.astype(jnp.float32)[:, :, None]
    left_projection = (
        (
            jnp.einsum(
                "rdz,zg->rdg",
                outer_normalized,
                tensor_product_matrix[:, :outer_factor_width],
                preferred_element_type=jnp.float32,
            )
            * alignment_mask_rows
        )
        .astype(jnp.bfloat16)
        .reshape(sequence_total, residue_total * outer_factor_width)
    )
    right_projection = (
        (
            jnp.einsum(
                "rdz,zg->rdg",
                outer_normalized,
                tensor_product_matrix[:, outer_factor_width:],
                preferred_element_type=jnp.float32,
            )
            * alignment_mask_rows
        )
        .astype(jnp.bfloat16)
        .reshape(sequence_total, residue_total * outer_factor_width)
    )
    left_gathered, right_gathered = (
        lax.all_gather(left_projection, ("branch", "chan"), axis=0, tiled=True),
        lax.all_gather(right_projection, ("branch", "chan"), axis=0, tiled=True),
    )
    column_index = lax.axis_index("branch") * lax.axis_size("chan") + lax.axis_index("chan")
    right_block = lax.dynamic_slice_in_dim(
        right_gathered,
        column_index * (column_block * outer_factor_width),
        column_block * outer_factor_width,
        1,
    )
    left_block = lax.all_to_all(left_gathered, "dap", split_axis=1, concat_axis=0, tiled=True)
    right_full = lax.all_gather(right_block, "dap", axis=0, tiled=True)
    total_seqs = left_block.shape[0]
    outer = jnp.einsum(
        "sic,sjd->ijcd",
        left_block.reshape(total_seqs, rows_block, outer_factor_width),
        right_full.reshape(total_seqs, column_block, outer_factor_width),
        preferred_element_type=jnp.float32,
    ) * (1.0 / total_seqs)
    flat_outer = outer.astype(jnp.bfloat16).reshape(
        rows_block * column_block, outer_factor_width * outer_factor_width
    )
    outer_update = jnp.dot(
        flat_outer, outer_output_weight, preferred_element_type=jnp.float32
    ).reshape(rows_block, column_block, pair_width)
    pair_activation_output = (
        pair_activation_input.astype(jnp.float32) + tri_update + outer_update
    ).astype(jnp.bfloat16)
    return (alignment_output, pair_activation_output)


LANES = 128
SUB = 8
LOG2E = 1.4426950408889634


def dot_nn(left, right):
    return lax.dot_general(left, right, (((1,), (0,)), ((), ())), preferred_element_type=jnp.float32)


def dot_nt(left, right):
    return lax.dot_general(left, right, (((1,), (1,)), ((), ())), preferred_element_type=jnp.float32)


def chunk_swap(parts, width):
    parts = list(parts)
    lane = lax.broadcasted_iota(jnp.int32, parts[0].shape, parts[0].ndim - 1)
    axis = parts[0].ndim - 1
    step = len(parts) // 2
    while step >= 1:
        span = step * width
        low = (lane // span) % 2 == 0
        for a in range(len(parts)):
            if (a // step) % 2 == 0:
                lo, hi = parts[a], parts[a + step]
                parts[a] = jnp.where(low, lo, pltpu.roll(hi, span, axis))
                parts[a + step] = jnp.where(low, pltpu.roll(lo, LANES - span, axis), hi)
        step //= 2
    return parts


def norm_rows(values, gain):
    center = values - jnp.mean(values, axis=-1, keepdims=True)
    spread = jnp.mean(center * center, axis=-1, keepdims=True)
    return center * lax.rsqrt(spread + 1e-05) * gain


def half_sigmoid(values):
    return 0.5 * jnp.tanh(0.5 * values) + 0.5


def wide_stat(parts, ones, width):
    total = sum(dot_nn(x, ones) for x in parts) * (1.0 / width)
    return jnp.concatenate([total] * (width // LANES), axis=1)


def norm_mxu(values, parts, gain, ones):
    width = values.shape[1]
    center = values - wide_stat(parts, ones, width)
    spread = wide_stat([(center * center).astype(jnp.bfloat16)], ones, width)
    return center * lax.rsqrt(spread + 1e-05) * gain


def staged_kernel(sizes, order, *refs):
    count = len(order)
    sources, rest = refs[:count], refs[count : len(refs) - count - 1]
    held, sems = refs[len(refs) - count - 1 : -1], refs[-1]
    fetches = [pltpu.make_async_copy(sources[i], held[i], sems.at[i]) for i in range(count)]

    def begin():
        for i in order:
            fetches[i].start()

    def ready(*which):
        for i in which:
            fetches[i].wait()

    block_kernel(sizes, begin, ready, *held, *rest)


def block_kernel(
    sizes,
    begin,
    ready,
    feat,
    tokens,
    amask,
    pair,
    pmask,
    table,
    focus_gain,
    entry,
    exit_w,
    pair_gain,
    head_t,
    product_gain,
    prod_t,
    outer_w,
    tri_w,
    tri_gain,
    tri_out,
    align_out,
    pair_out,
    pn,
    bsend,
    brecv,
    tsend,
    trecv_l,
    trecv_r,
    lsend,
    rsend,
    lrecv,
    rrecv,
    zsend,
    zrecv,
    stage_a,
    stage_b,
    stage_z,
    bias_full,
    emb,
    qd,
    keys,
    entry_t,
    vt,
    rows_n,
    att_t,
    mask_c,
    gates,
    normed,
    w2t,
    upd,
    rblk,
    obuf,
    table_f,
    left_w,
    gate_f,
    b_send,
    b_z,
    b_x,
    b_c,
    t_send,
    t_recv,
    o_send,
    o_recv,
    o_z,
    o_f,
    z_send,
    z_recv,
    l_send,
    l_z,
    l_recv,
    row_in,
):
    P_, B_, K_ = sizes
    Q_ = B_ * K_
    D_ = P_ * Q_
    rows, cols, cz = pair.shape
    seqs, res, width = feat.shape
    heads = head_t.shape[0]
    hw = width // heads
    per = LANES // hw
    groups = width // LANES
    fac = prod_t.shape[0] // 2
    nch = LANES // cols
    G = rows // nch
    mp = lax.axis_index("dap")
    mb = lax.axis_index("branch")
    mk = lax.axis_index("chan")
    mq = mb * K_ + mk
    me = mp * Q_ + mq

    def peer(off):
        dp, db, dk = off // Q_, (off // K_) % B_, off % K_
        p, b, k = mp ^ dp, mb ^ db, mk ^ dk
        return p, b * K_ + k, {"dap": p, "branch": b, "chan": k}

    def remote(src, dst, ss, rs, dev):
        return pltpu.make_async_remote_copy(
            src_ref=src,
            dst_ref=dst,
            send_sem=ss,
            recv_sem=rs,
            device_id=dev,
            device_id_type=pl.DeviceIdType.MESH,
        )

    here_dev = peer(1)[2]

    def sent(ref, sem):
        remote(ref, ref, sem, sem, here_dev).wait_send()

    def arrived(ref, sem):
        remote(ref, ref, sem, sem, here_dev).wait_recv()

    def exchange(send, recv, ss, rs, offs):
        for off in offs:
            p, q, dev = peer(off)
            remote(send(p, q), recv.at[me], ss, rs, dev).start()

    z_offs = [op * Q_ for op in range(1, P_)]
    q_offs = list(range(1, Q_))
    all_offs = sorted(range(1, D_), key=lambda off: (-(off // Q_), off % Q_))

    half_p = P_ // 2
    begin()
    barrier = pltpu.get_barrier_semaphore()
    for off in z_offs + q_offs:
        pl.semaphore_signal(
            barrier, inc=1, device_id=peer(off)[2], device_id_type=pl.DeviceIdType.MESH
        )

    ready(3, 9)
    pair_h = pair[...].reshape(rows * cols, cz)
    ones_z = jnp.ones((cz, LANES), jnp.bfloat16)
    pn[...] = norm_mxu(pair_h.astype(jnp.float32), [pair_h], pair_gain[...], ones_z).astype(
        jnp.bfloat16
    )

    def pair_rows(g):
        return jnp.concatenate(
            [pn[(a * G + g) * cols : (a * G + g + 1) * cols, :] for a in range(nch)], axis=0
        )

    ready(10)
    for g in range(G):
        stage_b[g * heads : (g + 1) * heads, :] = dot_nt(head_t[...], pair_rows(g)) * LOG2E
    for b in range(groups):
        pieces = []
        for h in range(per):
            by_head = stage_b[pl.ds(b * per + h, G, stride=heads), :]
            for a in range(nch):
                pieces.append(pltpu.roll(by_head, LANES - a * cols, 1) if a else by_head)
        bsend[b * cols : (b + 1) * cols, :] = jnp.concatenate(pieces, axis=0).T[:cols]
    brecv[me] = bsend[...]
    pl.semaphore_wait(barrier, P_ + Q_ - 2)
    for off in z_offs:
        pl.semaphore_signal(
            row_in, inc=1, device_id=peer(off)[2], device_id_type=pl.DeviceIdType.MESH
        )
    for op in range(1, P_):
        p, q, dev = peer(op * Q_)
        remote(bsend, brecv.at[me], b_send, b_z.at[op], dev).start()
    xoff = K_

    def pass_on(src, slot, sem, off):
        remote(src, brecv.at[slot], b_send, sem, peer(off)[2]).start()

    pass_on(bsend, me, b_x.at[0], xoff)
    pass_on(bsend, me, b_c, 1)
    owners = half_p * Q_
    parts_n = 2
    per_dev = cz // (owners * parts_n)
    unit = G * per_dev
    mine = (mp % half_p) * Q_ + mq
    ready(4, 14)
    mrows = jnp.concatenate(
        [pmask[a * G : (a + 1) * G, :].astype(jnp.float32) for a in range(nch)], axis=1
    )
    trecv = (trecv_l, trecv_r)

    def tri_factor(side):
        at = 2 * side * cz
        tri_t = tri_w[:, at : at + 2 * cz].astype(jnp.float32).T.astype(jnp.bfloat16)
        for t in range(G // 2):
            block = jnp.concatenate([pair_rows(2 * t), pair_rows(2 * t + 1)], axis=0)
            lin = dot_nt(tri_t, block)
            mrow = jnp.concatenate([mrows[2 * t : 2 * t + 1], mrows[2 * t + 1 : 2 * t + 2]], axis=1)
            val = half_sigmoid(lin[cz:]) * (lin[:cz] * mrow)
            for n in range(owners):
                for h in range(parts_n):
                    at_c = (n * parts_n + h) * per_dev
                    piece = val[at_c : at_c + per_dev]
                    two = jnp.concatenate([piece[:, :LANES], piece[:, LANES:]], axis=0)
                    tsend[side, h, n, 2 * t * per_dev : 2 * (t + 1) * per_dev, :] = two.astype(
                        jnp.bfloat16
                    )
        for h in range(parts_n):
            if side == 0:
                trecv_l[h, mine] = tsend[side, h, mine]
            else:
                trecv_r[h, me] = tsend[side, h, mine]

    def tri_send(side, h, offs):
        for off in offs:
            p, q, dev = peer(off)
            slot = mine if side == 0 else me
            remote(
                tsend.at[side, h, (p % half_p) * Q_ + q],
                trecv[side].at[h, slot],
                t_send.at[side],
                t_recv.at[side, h],
                dev,
            ).start()

    in_half = [off for off in range(1, D_) if off // Q_ < half_p]
    far = [off for off in range(1, D_) if off // Q_ >= half_p]
    own_row = [off for off in in_half if off < Q_]
    next_row = [off for off in in_half if off >= Q_]
    same_x = lambda offs: [off for off in offs if (off // K_) % B_ == 0]
    other_x = lambda offs: [off for off in offs if (off // K_) % B_ == 1]
    tri_factor(1)
    for h in range(parts_n):
        tri_send(1, h, [off for off in far if off in z_offs])
    pl.semaphore_wait(row_in, P_ - 1)
    for h in range(parts_n):
        tri_send(1, h, [off for off in same_x(far) if off not in z_offs])
    tri_factor(0)
    for h in range(parts_n):
        tri_send(1, h, in_half)
        tri_send(0, h, in_half)

    ready(0, 1, 2, 5, 6, 7, 8, 11, 12, 13, 15, 16)
    table_f[...] = jnp.zeros_like(table_f)
    table_f[: table.shape[0], :] = table[...].astype(jnp.float32)
    table_all = table_f[...].astype(jnp.bfloat16)
    kinds_n = table_f.shape[0]
    ones_m = jnp.ones((width, LANES), jnp.bfloat16)
    scale = hw ** (-0.5) * LOG2E
    for n, at in enumerate((0, 2 * width, 3 * width)):
        part = entry[:, at : at + width].astype(jnp.float32).T
        entry_t[n * width : (n + 1) * width, :] = part.astype(jnp.bfloat16)
    qd[...] = jnp.zeros_like(qd)
    for s in range(seqs):
        for h in range(heads):
            vt[s, h, hw:, :] = jnp.ones((vt.shape[2] - hw, res), jnp.bfloat16)
    kinds = lax.broadcasted_iota(jnp.int32, (kinds_n, res), 0)
    hot = jnp.concatenate(
        [jnp.where(kinds == tokens[s : s + 1, :], 1.0, 0.0) for s in range(seqs)], axis=1
    ).astype(jnp.float32)
    here = feat[...].astype(jnp.float32).reshape(seqs * res, width)
    here = here + dot_nn(hot.T.astype(jnp.bfloat16), table_all)
    emb[...] = here
    high = here.astype(jnp.bfloat16)
    low = (here - high.astype(jnp.float32)).astype(jnp.bfloat16)
    rows_n[...] = norm_mxu(here, [high, low], focus_gain[...], ones_m).astype(jnp.bfloat16)
    keys[...] = dot_nn(rows_n[...], entry[:, width : 2 * width]).astype(jnp.bfloat16)
    for u in range(seqs // 2):
        two = rows_n[2 * u * res : 2 * (u + 1) * res, :]
        for n in range(3):
            turned = dot_nt(entry_t[n * width : (n + 1) * width, :], two)
            for v in range(2):
                s = 2 * u + v
                here = turned[:, v * res : (v + 1) * res]
                if n == 2:
                    gates[s] = half_sigmoid(here)
                    continue
                for h in range(heads):
                    b, e = h // per, h % per
                    part = here[h * hw : (h + 1) * hw]
                    if n == 0:
                        qd[s, b, e * hw : (e + 1) * hw, e * res : (e + 1) * res] = (
                            part * scale
                        ).astype(jnp.bfloat16)
                    else:
                        vt[s, h, :hw, :] = part.astype(jnp.bfloat16)

    for op in range(1, P_):
        arrived(bsend, b_z.at[op])
        slot = (mp ^ op) * Q_ + mq
        pass_on(brecv.at[slot], slot, b_x.at[op], xoff)
        pass_on(brecv.at[slot], slot, b_c, 1)
    for h in range(parts_n):
        tri_send(1, h, other_x(far))

    four = jnp.concatenate([prod_t[:fac, :].astype(jnp.float32)] * nch, axis=0).T
    lane_fac = lax.broadcasted_iota(jnp.int32, four.shape, 1) // fac
    for a in range(nch):
        left_w[a * width : (a + 1) * width, :] = jnp.where(lane_fac == a, four, 0.0).astype(
            jnp.bfloat16
        )
    for g in range(G):
        gate_f[g] = half_sigmoid(dot_nn(pair_rows(g), tri_w[:, 4 * cz :]))
    stage_a[...] = outer_w[...].astype(jnp.float32)
    for g in range(SUB):
        piece = jnp.concatenate(
            [stage_a[pl.ds(a * SUB + g, fac, stride=fac), :] for a in range(fac // SUB)], axis=0
        )
        w2t[:, g * LANES : (g + 1) * LANES] = piece.T.astype(jnp.bfloat16)

    for op in range(P_):
        arrived(bsend, b_x.at[op])
        slot = (mp ^ op) * Q_ + (mb ^ 1) * K_ + mk
        pass_on(brecv.at[slot], slot, b_c, 1)
    arrived(brecv.at[: 2 * P_], b_c)
    for q in range(Q_):
        for b in range(groups):
            got = chunk_swap(
                [brecv[p * Q_ + q, b * cols : (b + 1) * cols, :] for p in range(P_)], cols
            )
            for h in range(per):
                bias_full[b, q * cols : (q + 1) * cols, h * res : (h + 1) * res] = got[h]

    for s in range(seqs):
        mcol = jnp.broadcast_to(amask[s : s + 1, :].astype(jnp.float32), (res, res)).T
        mask_add = (mcol - 1.0) * (1000000000.0 * LOG2E)
        for h in range(heads):
            b, e = h // per, h % per
            sl = slice(e * res, (e + 1) * res)
            sc = dot_nn(
                keys[s * res : (s + 1) * res, b * LANES : (b + 1) * LANES], qd[s, b, :, sl]
            )
            sc = (sc + bias_full[b, :, sl]) + mask_add
            ex = jnp.exp2(sc - jnp.max(sc, axis=0, keepdims=True)).astype(jnp.bfloat16)
            av = dot_nn(vt[s, h], ex)
            att_t[h * hw : (h + 1) * hw, s * res : (s + 1) * res] = (
                av[:hw] * (1.0 / av[hw : hw + 1]) * gates[s, h * hw : (h + 1) * hw, :]
            )
        mask_c[s * res : (s + 1) * res, :] = mcol
    attended = att_t[...].T.astype(jnp.bfloat16)
    out = (emb[...] + dot_nn(attended, exit_w[...])).astype(jnp.bfloat16)
    align_out[...] = out.reshape(seqs, res, width)
    on = norm_mxu(out.astype(jnp.float32), [out], product_gain[...], ones_m)
    on = on.astype(jnp.bfloat16).astype(jnp.float32)
    for b in range(groups):
        normed[b] = on[:, b * LANES : (b + 1) * LANES] * mask_c[...]

    each = seqs * res // nch
    wide = [
        normed[b, pl.ds(a, each, stride=nch), :].astype(jnp.bfloat16)
        for a in range(nch)
        for b in range(groups)
    ]
    left = dot_nn(jnp.concatenate(wide, axis=1), left_w[...])
    rows_all = jnp.concatenate([normed[b] for b in range(groups)], axis=1).astype(jnp.bfloat16)
    right = dot_nt(prod_t[fac:, :], rows_all)
    lefts = [
        jnp.concatenate(
            [left[(s * P_ + p) * G : (s * P_ + p + 1) * G] for s in range(seqs)], axis=0
        ).astype(jnp.bfloat16)
        for p in range(P_)
    ]
    by_seq = []
    for s in range(seqs):
        by_seq.append(
            chunk_swap(
                [right[a * SUB : (a + 1) * SUB, s * res : (s + 1) * res] for a in range(nch)], cols
            )
        )
    half = seqs * SUB
    for p in range(P_):
        lsend[p] = lefts[p]
    for q in range(Q_):
        rsend[q] = jnp.concatenate([by_seq[s][q] for s in range(seqs)], axis=0).astype(jnp.bfloat16)
    lrecv[me] = lsend[mp]
    rrecv[me] = rsend[mq]
    for op in range(1, P_):
        p, q, dev = peer(op * Q_)
        remote(lsend.at[p], lrecv.at[me], l_send, l_z.at[op], dev).start()
    exchange(lambda p, q: lsend.at[mp], lrecv, l_send, l_recv, q_offs)
    cross = [off for off in all_offs if off // Q_ == half_p]
    exchange(lambda p, q: rsend.at[q], rrecv, o_send, o_z, cross)
    exchange(lambda p, q: rsend.at[q], rrecv, o_send, o_recv, [off for off in all_offs if off // Q_ < half_p])

    def tri_sums(h):
        for side, stage in enumerate((stage_a, stage_b)):
            arrived(trecv[side].at[h, : (owners if side == 0 else D_) - 1], t_recv.at[side, h])
            for p in range(half_p if side == 0 else P_):
                got = chunk_swap(
                    [trecv[side][h, p * Q_ + q].astype(jnp.float32) for q in range(Q_)],
                    cols,
                )
                for a in range(nch):
                    stage[(p * nch + a) * unit : (p * nch + a + 1) * unit, :] = got[a]
        for c in range(per_dev):
            lc = stage_a[pl.ds(c, half_p * rows, stride=per_dev), :].astype(jnp.bfloat16)
            rc = stage_b[pl.ds(c, res, stride=per_dev), :].astype(jnp.bfloat16)
            z = dot_nt(lc, rc)
            for p in range(half_p):
                got = chunk_swap(
                    [z[(p * nch + a) * G : (p * nch + a + 1) * G] for a in range(nch)], cols
                )
                for q in range(Q_):
                    stage_z[pl.ds((p * Q_ + q) * unit + c, G, stride=per_dev), :] = got[q]
        for n in range(owners):
            zsend[h, n] = stage_z[n * unit : (n + 1) * unit, :].astype(jnp.bfloat16)
        zrecv[h, mine] = zsend[h, mine]
        for off in sorted(in_half, reverse=True):
            p, q, dev = peer(off)
            remote(
                zsend.at[h, (p % half_p) * Q_ + q], zrecv.at[h, mine], z_send, z_recv.at[h], dev
            ).start()

    for h in range(parts_n):
        tri_sums(h)
        if h == 0:
            for op in range(1, P_):
                arrived(lsend.at[0], l_z.at[op])
                slot = (mp ^ op) * Q_ + mq
                for off in q_offs:
                    remote(
                        lrecv.at[slot], lrecv.at[slot], l_send, l_recv, peer(off)[2]
                    ).start()
            arrived(rrecv.at[:Q_], o_z)
            theirs = pl.ds((mp ^ half_p) * Q_, Q_)
            remote(rrecv.at[theirs], rrecv.at[theirs], o_send, o_f, peer(Q_)[2]).start()

    arrived(lrecv.at[: P_ * (Q_ - 1)], l_recv)
    arrived(rrecv.at[: half_p * Q_ - 1], o_recv)
    arrived(rrecv.at[:Q_], o_f)
    total = D_ * half
    for n in range(D_):
        stage_a[n * half : (n + 1) * half, :] = lrecv[n].astype(jnp.float32)
        stage_b[n * half : (n + 1) * half, :] = rrecv[n].astype(jnp.float32)
    seq_all = D_ * seqs
    gh = G // nch
    lhs = jnp.concatenate(
        [
            jnp.concatenate(
                [stage_a[pl.ds(a * gh + h, seq_all, stride=SUB), :] for a in range(nch)], axis=0
            ).T
            for h in range(gh)
        ],
        axis=0,
    ).astype(jnp.bfloat16)
    lane_col = lax.broadcasted_iota(jnp.int32, (seq_all, LANES), 1) // cols
    keep = [jnp.where(lane_col == a, 1.0, 0.0).astype(jnp.bfloat16) for a in range(nch)]
    for k in range(SUB):
        here = stage_b[pl.ds(k, seq_all, stride=SUB), :]
        turned = [here] + [pltpu.roll(here, r * cols, 1) for r in range(1, nch)]
        turned = [x.astype(jnp.bfloat16) for x in turned]
        for d in range(nch):
            at = (k * nch + d) * LANES
            for a in range(nch):
                rblk[a * seq_all : (a + 1) * seq_all, at : at + LANES] = (
                    turned[(a - d) % nch] * keep[a]
                )
        for t in range(k * nch // 2, (k + 1) * nch // 2):
            prod = dot_nn(lhs, rblk[:, 2 * t * LANES : 2 * (t + 1) * LANES]).astype(jnp.bfloat16)
            for g in range(G):
                for e in range(2):
                    obuf[g // 2, (2 * t + e) * fac : (2 * t + e + 1) * fac, (g % 2) * LANES : (g % 2 + 1) * LANES] = prod[
                        g * fac : (g + 1) * fac, e * LANES : (e + 1) * LANES
                    ]
    for t in range(G // 2):
        both = dot_nn(w2t[...], obuf[t]) * (1.0 / seq_all)
        for e in range(2):
            g = 2 * t + e
            up = both[:, e * LANES : (e + 1) * LANES].T
            for a in range(nch):
                sl = slice(a * cols, (a + 1) * cols)
                upd[g, sl, :] = pair[a * G + g].astype(jnp.float32) + up[sl]

    sent(brecv.at[: D_ - 1], b_send)
    sent(trecv_l.at[:, : owners - 1], t_send.at[0])
    sent(trecv_r.at[:, : D_ - 1], t_send.at[1])
    sent(lrecv.at[: D_ - 1], l_send)
    sent(rrecv.at[: D_ - 1], o_send)
    for h in range(parts_n):
        arrived(zrecv.at[h, : owners - 1], z_recv.at[h])
    for n in range(owners):
        for h in range(parts_n):
            at_c = (n * parts_n + h) * unit
            stage_a[at_c : at_c + unit, :] = zrecv[h, n].astype(jnp.float32)
    for g in range(G):
        sums_g = jnp.concatenate(
            [
                stage_a[n * unit + g * per_dev : n * unit + (g + 1) * per_dev, :]
                for n in range(owners * parts_n)
            ],
            axis=0,
        ).T
        tn = norm_rows(sums_g, tri_gain[...]).astype(jnp.bfloat16)
        both = upd[g] + gate_f[g] * dot_nn(tn, tri_out[...])
        for a in range(nch):
            i = a * G + g
            sl = slice(a * cols, (a + 1) * cols)
            pair_out[i] = both[sl].astype(jnp.bfloat16)
    sent(zrecv.at[:, : owners - 1], z_send)


def settle_kernel(one, two, one_out, two_out, one_held, two_held, sems):
    come = [
        pltpu.make_async_copy(one, one_held, sems.at[0]),
        pltpu.make_async_copy(two, two_held, sems.at[1]),
    ]
    go = [
        pltpu.make_async_copy(one_held, one_out, sems.at[2]),
        pltpu.make_async_copy(two_held, two_out, sems.at[3]),
    ]
    for c in come:
        c.start()
    for c, d in zip(come, go):
        c.wait()
        d.start()
    for d in go:
        d.wait()


def kernel_fits(P_, B_, K_, args):
    Q_ = B_ * K_
    feat, pair, head_w, prod_w = args[0], args[3], args[10], args[12]
    rows, cols, cz = pair.shape
    seqs, res, width = feat.shape
    heads = head_w.shape[1]
    fac = prod_w.shape[1] // 2
    nch = LANES // cols
    return (
        res == LANES
        and cz == LANES
        and rows == cols
        and fac == cols
        and nch == P_
        and nch == Q_
        and rows == nch * SUB
        and cz == P_ * Q_ * SUB
        and heads == SUB
        and width % LANES == 0
        and width // heads == cols
        and D_rows(P_, Q_, seqs) <= fac * fac
        and P_ == 4
        and B_ == 2
        and K_ == 2
    )


def D_rows(P_, Q_, seqs):
    return P_ * Q_ * seqs * SUB


def fused(*args):
    P_ = lax.axis_size("dap")
    B_ = lax.axis_size("branch")
    K_ = lax.axis_size("chan")
    Q_ = B_ * K_
    D_ = P_ * Q_
    if not kernel_fits(P_, B_, K_, args):
        return shards(*args)
    (feat, tokens, amask, pair, pmask, table, focus_gain, entry, exit_w, pair_gain, head_w) = args[:11]
    (product_gain, prod_w, outer_w, tri_w, tri_gain, tri_out) = args[11:]
    rows, cols, cz = pair.shape
    seqs, res, width = feat.shape
    heads = head_w.shape[1]
    fac = prod_w.shape[1] // 2
    nch = LANES // cols
    G = rows // nch
    per = LANES // (width // heads)
    operands = (
        feat,
        tokens,
        amask,
        pair,
        pmask,
        table,
        focus_gain[None, :],
        entry,
        exit_w,
        pair_gain[None, :],
        head_w.T,
        product_gain[None, :],
        prod_w.T,
        outer_w,
        tri_w,
        tri_gain[None, :],
        tri_out,
    )
    order = (3, 9, 10, 14, 4, 0, 1, 5, 6, 7, 13, 12, 2, 8, 11, 15, 16)
    owners = P_ // 2 * Q_
    parts_n = 2
    per_dev = cz // (owners * parts_n)
    unit = G * per_dev
    half = seqs * SUB
    seq_all = D_ * seqs
    f32, bf16 = jnp.float32, jnp.bfloat16
    vm = pltpu.VMEM
    dma = pltpu.SemaphoreType.DMA
    results = pl.pallas_call(
        functools.partial(staged_kernel, (P_, B_, K_), order),
        out_shape=(
            jax.ShapeDtypeStruct(feat.shape, bf16),
            jax.ShapeDtypeStruct(pair.shape, bf16),
        ),
        in_specs=[pl.BlockSpec(memory_space=pltpu.HBM)] * len(operands),
        out_specs=(pl.BlockSpec(memory_space=vm), pl.BlockSpec(memory_space=vm)),
        scratch_shapes=[
            vm((rows * cols, cz), bf16),
            vm((G * heads, LANES), f32),
            vm((D_, G * heads, LANES), f32),
            vm((2, parts_n, owners, unit, LANES), bf16),
            vm((parts_n, owners, unit, LANES), bf16),
            vm((parts_n, D_, unit, LANES), bf16),
            vm((P_, half, LANES), bf16),
            vm((Q_, half, LANES), bf16),
            vm((D_, half, LANES), bf16),
            vm((D_, half, LANES), bf16),
            vm((parts_n, owners, unit, LANES), bf16),
            vm((parts_n, owners, unit, LANES), bf16),
            vm((fac * fac, LANES), f32),
            vm((fac * fac, LANES), f32),
            vm((owners * unit, LANES), f32),
            vm((width // LANES, res, per * res), f32),
            vm((seqs * res, width), f32),
            vm((seqs, width // LANES, LANES, per * res), bf16),
            vm((seqs * res, width), bf16),
            vm((3 * width, width), bf16),
            vm((seqs, heads, width // heads + 16, res), bf16),
            vm((seqs * res, width), bf16),
            vm((width, seqs * res), f32),
            vm((seqs * res, LANES), f32),
            vm((seqs, width, res), f32),
            vm((width // LANES, seqs * res, LANES), f32),
            vm((cz, fac * fac), bf16),
            vm((G, LANES, LANES), f32),
            vm((nch * seq_all, fac * LANES), bf16),
            vm((G // 2, fac * fac, 2 * LANES), bf16),
            vm((-(-table.shape[0] // 16) * 16, width), f32),
            vm((nch * width, nch * fac), bf16),
            vm((G, LANES, cz), f32),
            dma,
            dma((P_,)),
            dma((P_,)),
            dma,
            dma((2,)),
            dma((2, parts_n)),
            dma,
            dma,
            dma,
            dma,
            dma,
            dma((parts_n,)),
            dma,
            dma((P_,)),
            dma,
            pltpu.SemaphoreType.REGULAR,
        ]
        + [vm(x.shape, x.dtype) for x in operands]
        + [dma((len(operands),))],
        compiler_params=pltpu.CompilerParams(collective_id=0, has_side_effects=True),
    )(*operands)
    return pl.pallas_call(
        settle_kernel,
        out_shape=tuple(jax.ShapeDtypeStruct(x.shape, x.dtype) for x in results),
        in_specs=[pl.BlockSpec(memory_space=pltpu.HBM)] * 2,
        out_specs=(pl.BlockSpec(memory_space=pltpu.HBM),) * 2,
        scratch_shapes=[vm(x.shape, x.dtype) for x in results] + [dma((4,))],
    )(*results)


def solution(mesh):
    in_specs = (
        P(("groups", "dap", "branch", "chan"), None, None),
        P(("groups", "dap", "branch", "chan"), None),
        P(("groups", "dap", "branch", "chan"), None),
        P(("groups", "dap"), ("branch", "chan"), None),
        P(("groups", "dap"), ("branch", "chan")),
        P(),
        P(),
        P(),
        P(),
        P(),
        P(),
        P(),
        P(),
        P(),
        P(),
        P(),
        P(),
    )
    out_specs = (
        P(("groups", "dap", "branch", "chan"), None, None),
        P(("groups", "dap"), ("branch", "chan"), None),
    )
    return jax.shard_map(fused, mesh=mesh, in_specs=in_specs, out_specs=out_specs, check_vma=False)
```
